512 devices in a mesh: grp: 8 (over y), inner: 64 (over z, x, core).
Axes of the slice: x: 4, y: 8, z: 8, core: 2. Of those that a mesh axis runs over, the one named last changes fastest.
Arguments:
- row_left: bfloat16 [256, 1024, 128], P('inner', 'grp'), may hold values from -6 to 6
- row_right: bfloat16 [256, 1024, 128], P('inner', 'grp'), may hold values from -0.1875 to 0.1875
- col_left: bfloat16 [256, 1024, 2048], P('inner', None, 'grp'), may hold values from -6 to 6
- col_right: bfloat16 [256, 1024, 2048], P('inner', None, 'grp'), may hold values from -0.1875 to 0.1875
- sketch_cols: bfloat16 [1024, 2048], P(None, 'grp'), may hold values from -6 to 6
- target_left: bfloat16 [1024, 2048], P('inner', 'grp'), may hold values from -6 to 6
- target_right: bfloat16 [1024, 2048], P('inner', 'grp'), may hold values from -24 to 24
- live_counts: int32 [64], P('inner'), may hold values from 1 to 4, 160 in all
Outputs:
- new_basis: float32 [1024, 2048], P('inner', 'grp')
- new_coeffs: float32 [1024, 2048], P('inner', 'grp')
The draws below stay inside these ranges and needn't reach their ends.
Inputs may be any that keep to these rules, and one draw needn't show every extreme that they name: Member m uses its first live_counts[m] slots; data in other slots is read by no output. Some member uses all 4 slots, and the counts sum to (5) times the number of members, halved.
All inputs are finite; a program needn't handle non-finite values. No bound on the sum of `live_counts` on one device may be relied on, other than what follows from the above.
Results may differ from the reference program's by a relative error of at most 0.0042.
Values may be sent and summed in bfloat16 or wider, within the bound.
No kernel may reach another device: no remote copies, remote signals or barrier semaphores. Data moves between devices by JAX's collectives and lax.ppermute only.
A program may use at most 64 MiB of HBM per device.

```python
import math
import jax
import jax.numpy as jnp
import numpy as np
from jax import lax

TILE = 1024
RANK = 128
K_DEV = 4
MEMBERS = 64
SLOTS = 256
TARGETS = 16
N_INNER = 64


def level_of(key, extent, pieces, smallest, high):
    gain = 1.0
    for position, shards_of in pieces:
        draws = jax.random.uniform(jax.random.fold_in(jax.random.fold_in(key, 6), position), (shards_of,), jnp.float32, smallest / len(pieces), high / len(pieces))
        gain = gain * jnp.repeat(jnp.exp(draws), extent[position] // shards_of).reshape((-1,) + (1,) * (len(extent) - 1 - position))
    return gain


def length_profile(amount, total, reach, lean):
    loads = [(1 << 20) // math.isqrt(standing ** lean) + 1 for standing in range(2, amount + 1)]
    surplus, counts = total - reach - (amount - 1), [1] * (amount - 1)
    while surplus > 0:
        candidates = [i for i in range(amount - 1) if counts[i] < reach]
        mass, left = sum([loads[i] for i in candidates]), surplus
        for i in candidates:
            more = min(reach - counts[i], max(1, left * loads[i] // mass), surplus)
            counts[i] = counts[i] + more
            surplus = surplus - more
    return np.array([reach] + counts)


def uneven_parts(own_key, number_of, total, limit, slope):
    if number_of == 2:
        one = jax.random.randint(own_key, (), max(1, total - limit), min(limit, total - 1) + 1)
        return jnp.stack([one, total - one])
    sizes = jnp.asarray(length_profile(number_of, total, limit, slope), jnp.int32)
    twos = (number_of - 1) // 2
    source_of, sink = sizes[1:1 + 2 * twos:2], sizes[2:2 + 2 * twos:2]
    margin = jnp.minimum(source_of - 1, limit - sink)
    passed = jax.random.randint(jax.random.fold_in(own_key, 1), (twos,), 0, 1 << 20) % (margin + 1)
    sizes = sizes.at[1:1 + 2 * twos:2].set(source_of - passed).at[2:2 + 2 * twos:2].set(sink + passed)
    return sizes[jax.random.permutation(jax.random.fold_in(own_key, 2), number_of)]


def bell_draw(own_key, extent, spread, reach, cuts=(), held_as=jnp.bfloat16):
    array = spread * jax.random.normal(own_key, extent, jnp.float32)
    if cuts:
        array = array * level_of(own_key, extent, cuts, -0.22, 0.18)
    return jnp.clip(array, -reach, reach).astype(held_as)


def setup_inputs(seed: int = 0) -> dict:
    key_list = jax.random.split(jax.random.key(seed), 9)
    row_left = bell_draw(key_list[0], (SLOTS, TILE, RANK), 1.0, 6.0, ((0, 64), (1, 8)))
    row_right = bell_draw(key_list[1], (SLOTS, TILE, RANK), TILE ** -0.5, 0.1875, ((0, 64), (1, 8)))
    col_left = bell_draw(key_list[2], (SLOTS, TILE, TARGETS * RANK), 1.0, 6.0, ((0, 64), (2, 8)))
    col_right = bell_draw(key_list[3], (SLOTS, TILE, TARGETS * RANK), TILE ** -0.5, 0.1875, ((0, 64), (2, 8)))
    sketch_cols = bell_draw(key_list[4], (TILE, TARGETS * RANK), 1.0, 6.0, ((1, 8),))
    target_left = bell_draw(key_list[5], (TILE, TARGETS * RANK), 1.0, 6.0, ((0, 64), (1, 8)))
    target_right = bell_draw(key_list[6], (TILE, TARGETS * RANK), 4.0, 24.0, ((0, 64), (1, 8)))
    live_counts = uneven_parts(key_list[7], MEMBERS, (K_DEV + 1) * N_INNER // 2, K_DEV, 2).astype(jnp.int32)
    return {"row_left": row_left, "row_right": row_right, "col_left": col_left, "col_right": col_right, "sketch_cols": sketch_cols, "target_left": target_left, "target_right": target_right, "live_counts": live_counts}


exact_accumulation = lax.Precision.HIGHEST

def orthonormal(sketched, gram):
    factor_low = jnp.linalg.cholesky(gram)
    blocks = jnp.transpose(sketched, (1, 2, 0))
    solved = jax.vmap(lambda tri, block: jax.scipy.linalg.solve_triangular(tri, block, lower=True))(factor_low, blocks)
    return jnp.transpose(solved, (2, 0, 1))

def rounded(values):
    low = lax.optimization_barrier(values.astype(jnp.bfloat16))
    return low.astype(jnp.float32)

def reference(row_left, row_right, col_left, col_right, sketch_cols, target_left, target_right, live_counts):
    tile_rows = sketch_cols.shape[0]
    low_rank = row_left.shape[2]
    targets = sketch_cols.shape[1] // low_rank
    both_width = targets * low_rank
    slot_ids = jnp.arange(row_left.shape[0], dtype=jnp.int32)
    live_mask = (slot_ids % K_DEV < live_counts[slot_ids // K_DEV]).astype(jnp.float32)
    sketch_partition = sketch_cols.astype(jnp.float32).reshape(tile_rows, targets, low_rank)
    left_split = target_left.astype(jnp.float32).reshape(tile_rows, targets, low_rank)
    right_split = target_right.astype(jnp.float32).reshape(tile_rows, targets, low_rank)

    def pair_core(slot_id):
        return jnp.dot(row_right[slot_id].T.astype(jnp.float32), col_right[slot_id].astype(jnp.float32), preferred_element_type=jnp.float32).reshape(low_rank, targets, low_rank)
    target_core = rounded(jnp.einsum('ntr,nts->trs', right_split, sketch_partition, precision=exact_accumulation))
    start_sum = jnp.einsum('ntr,trs->nts', left_split, target_core, precision=exact_accumulation).reshape(tile_rows, both_width)

    def forward(running, slot_id):
        pair = pair_core(slot_id)
        column_partition = col_left[slot_id].astype(jnp.float32).reshape(tile_rows, targets, low_rank)
        random_test_matrix = jnp.einsum('ntr,nts->trs', column_partition, sketch_partition, precision=exact_accumulation)
        mixed = jnp.einsum('rtq,tqs->rts', pair, random_test_matrix, precision=exact_accumulation) * live_mask[slot_id]
        mixed = mixed.astype(jnp.bfloat16).reshape(low_rank, both_width)
        return (running - jnp.dot(row_left[slot_id].astype(jnp.float32), mixed.astype(jnp.float32), preferred_element_type=jnp.float32), None)
    sketch_sum, _ = lax.scan(forward, start_sum, slot_ids)
    summed = sketch_sum.reshape(tile_rows, targets, low_rank)
    gram = jnp.einsum('ntr,nts->trs', summed, summed, precision=exact_accumulation) / tile_rows
    new_basis = orthonormal(summed, gram).reshape(tile_rows, both_width)
    basis_low = new_basis.astype(jnp.bfloat16)
    basis_split = lax.optimization_barrier(basis_low).astype(jnp.float32).reshape(tile_rows, targets, low_rank)
    target_back = rounded(jnp.einsum('ntr,nts->trs', left_split, basis_split, precision=exact_accumulation))
    start_back = jnp.einsum('ntr,trs->nts', right_split, target_back, precision=exact_accumulation).reshape(tile_rows, both_width)

    def reverse_pass(running, slot_id):
        pair = pair_core(slot_id)
        back = jnp.dot(row_left[slot_id].T.astype(jnp.float32), basis_low.astype(jnp.float32), preferred_element_type=jnp.float32).reshape(low_rank, targets, low_rank)
        collapsed_terms = (jnp.einsum('rtq,rts->qts', pair, back, precision=exact_accumulation) * live_mask[slot_id]).astype(jnp.bfloat16)
        column_partition = col_left[slot_id].astype(jnp.float32).reshape(tile_rows, targets, low_rank)
        term = jnp.einsum('ntq,qts->nts', column_partition, collapsed_terms.astype(jnp.float32), precision=exact_accumulation)
        return (running - term.reshape(tile_rows, both_width), None)
    coeff_sum, _ = lax.scan(reverse_pass, start_back, slot_ids)
    new_coeffs = coeff_sum / tile_rows
    return (new_basis, new_coeffs)
```

```python
import jax
import jax.numpy as jnp
from jax import lax
from jax.experimental import pallas as pl
from jax.experimental.pallas import tpu as pltpu
from jax.sharding import Mesh
from jax.sharding import PartitionSpec as P

INNER = ("inner_0", "inner_1", "inner_2")
LOW = jnp.bfloat16
FULL = jnp.float32


def dot(a, b, ca, cb):
    return lax.dot_general(a, b, (((ca,), (cb,)), ((), ())), preferred_element_type=FULL)


def halves(x):
    high = x.astype(LOW)
    return high, (x - high.astype(FULL)).astype(LOW)


def fine_dot(a, b, ca, cb):
    ah, al = halves(a)
    bh, bl = halves(b)
    return dot(ah, bh, ca, cb) + (dot(ah, bl, ca, cb) + dot(al, bh, ca, cb))


def inverse_factors(grams):
    n, count, block = grams[0].shape[0], len(grams), 64
    groups = block // 8
    eye = (
        lax.broadcasted_iota(jnp.int32, (n, n), 0) == lax.broadcasted_iota(jnp.int32, (n, n), 1)
    ).astype(FULL)
    sub = lax.broadcasted_iota(jnp.int32, (8, n), 0)
    left, right, done = list(grams), [eye] * count, [[] for _ in range(count)]
    for start in range(0, n, block):
        a = [[left[t][8 * g : 8 * g + 8] for g in range(groups)] for t in range(count)]
        b = [[right[t][8 * g : 8 * g + 8] for g in range(groups)] for t in range(count)]
        scale = [[jnp.ones((8, n), FULL) for g in range(groups)] for t in range(count)]
        for i in range(block):
            j, first, at = start + i, i // 8, i % 8
            for t in range(count):
                row_a = jnp.broadcast_to(a[t][first][at : at + 1, :], (8, n))
                row_b = jnp.broadcast_to(b[t][first][at : at + 1, :], (8, n))
                cols = [
                    jnp.broadcast_to(a[t][g][:, j : j + 1], (8, n)) for g in range(first, groups)
                ]
                root = lax.rsqrt(jnp.broadcast_to(cols[0][at : at + 1, :], (8, n)))
                row_a, row_b = row_a * (root * root), row_b * (root * root)
                scale[t][first] = jnp.where(sub == at, root, scale[t][first])
                for g in range(first, groups):
                    c = cols[g - first]
                    if g == first:
                        c = jnp.where(sub > at, c, 0.0)
                    a[t][g] = a[t][g] - c * row_a
                    b[t][g] = b[t][g] - c * row_b
        for t in range(count):
            rows_b = jnp.concatenate([b[t][g] * scale[t][g] for g in range(groups)], 0)
            done[t].append(rows_b)
            if start + block < n:
                rows_a = jnp.concatenate([a[t][g] * scale[t][g] for g in range(groups)], 0)
                ah, al = halves(rows_a)
                bh, bl = halves(rows_b)
                factor = jnp.concatenate([ah, ah, al], 0)
                cut_a = dot(factor, jnp.concatenate([ah, al, ah], 0), 0, 0)
                cut_b = dot(factor, jnp.concatenate([bh, bl, bh], 0), 0, 0)
                left[t] = left[t][block:] - cut_a[start + block :]
                right[t] = right[t][block:] - cut_b[start + block :]
    return [jnp.concatenate(rows, 0) for rows in done]


def probe_body(left_ref, sketch_ref, out_ref):
    for k in range(left_ref.shape[0]):
        for t in range(out_ref.shape[1]):
            cols = slice(128 * t, 128 * t + 128)
            out_ref[k, t] = dot(left_ref[k, :, cols], sketch_ref[:, cols], 0, 0)


def forward_body(
    place_ref, own, f1, b1, f2, b2, f3, b3, f4, b4,
    right_ref, probe_ref, tall_ref, tright_ref, sketch_ref,
    part_ref, pair_ref, pivot_ref, factor,
):
    group, live, groups = place_ref[0], place_ref[1], place_ref[2]
    slots = right_ref.shape[0]
    n = own.shape[1]

    def put(ref, first, distance, with_right, with_left):
        at = pl.multiple_of(lax.rem(group + distance, groups) * n, n)
        for k in range(slots):
            if with_right:
                factor[pl.ds(at, n), 128 * k : 128 * k + 128] = ref[k]
            if with_left:
                pivot_ref[pl.ds(at, n), 128 * k : 128 * k + 128] = ref[k + first]

    put(own, slots, 0, True, True)
    for s, (f, b) in enumerate(((f1, b1), (f2, b2), (f3, b3))):
        put(f, slots, groups - 1 - s, True, True)
        put(b, slots, 1 + s, True, True)
    put(f4, 0, 4, True, False)
    put(b4, 0, 4, False, True)
    mixed = []
    for k in range(slots):
        pair = dot(factor[:, 128 * k : 128 * k + 128], right_ref[k], 0, 0)
        pair_ref[k] = pair
        row = []
        for t in range(2):
            cols = slice(128 * t, 128 * t + 128)
            value = fine_dot(pair[:, cols], probe_ref[k, t], 1, 0)
            row.append(jnp.where(k < live, value, 0.0).astype(LOW))
        mixed.append(jnp.concatenate(row, 1))
    update = dot(pivot_ref[...], jnp.concatenate(mixed, 0), 1, 0)
    for t in range(2):
        cols = slice(128 * t, 128 * t + 128)
        core = dot(tright_ref[:, cols], sketch_ref[:, cols], 0, 0).astype(LOW)
        target = dot(tall_ref[:, cols], core, 1, 0)
        part_ref[:, cols] = (target - update[:, cols]).astype(LOW)


def backward_body(
    place_ref, all_ref, own_ref, pivot_ref, pair_ref, left_ref, tall_ref, tright_ref,
    basis_ref, term_ref, direct_ref,
):
    live = place_ref[1]
    slots, rows = left_ref.shape[0], all_ref.shape[0]
    turned, grams = [], []
    for t in range(2):
        s = all_ref[:, 128 * t : 128 * t + 128]
        grams.append(dot(s, s, 0, 0) / rows)
    inverse = inverse_factors(grams)
    for t in range(2):
        cols = slice(128 * t, 128 * t + 128)
        wh, wl = halves(inverse[t])
        s = all_ref[:, cols]
        basis = dot(wh, s, 1, 1) + dot(wl, s, 1, 1)
        turned = basis.astype(LOW)
        basis_ref[:, cols] = fine_dot(own_ref[:, cols], inverse[t], 1, 1)
        back = dot(turned, pivot_ref[...], 1, 0)
        total = None
        for k in range(slots):
            folded = fine_dot(back[:, 128 * k : 128 * k + 128], pair_ref[k, :, cols], 1, 0)
            folded = jnp.where(k < live, folded, 0.0).astype(LOW)
            term = dot(left_ref[k, :, cols], folded, 1, 1)
            total = term if total is None else total + term
        term_ref[:, cols] = (-total).astype(LOW)
        target_back = dot(turned, tall_ref[:, cols], 1, 0).astype(LOW)
        direct_ref[:, cols] = dot(tright_ref[:, cols], target_back, 1, 1)


SMEM = pl.BlockSpec(memory_space=pltpu.SMEM)
WHOLE = pl.BlockSpec()


def shift(x, axis, by):
    n = lax.axis_size(axis)
    return lax.ppermute(x, axis, [(i, (i + by) % n) for i in range(n)])


def to_all(x):
    n = lax.axis_size(INNER)
    return lax.all_to_all(jnp.broadcast_to(x[None], (n, *x.shape)), INNER, 0, 0, tiled=True)


def shards(
    row_left, row_right, col_left, col_right, sketch_cols, target_left, target_right, live_counts
):
    slots, rows, width = col_left.shape
    block = target_left.shape[0]
    n = lax.axis_size(INNER)
    place = jnp.stack(
        [lax.axis_index("grp"), live_counts[0], jnp.int32(lax.axis_size("grp"))]
    ).astype(jnp.int32)
    own = jnp.concatenate([row_right, row_left], 0)
    ups, downs, up, down = [], [], own, own
    for _ in range(3):
        up, down = shift(up, "grp", 1), shift(down, "grp", -1)
        ups.append(up)
        downs.append(down)
    ups.append(shift(up[:slots], "grp", 1))
    downs.append(shift(down[slots:], "grp", -1))
    all_left = to_all(target_left).reshape(rows, width)
    probe = pl.pallas_call(
        probe_body,
        out_shape=jax.ShapeDtypeStruct((slots, 2, 128, 128), FULL),
        name="probe",
    )(col_left, sketch_cols)
    own_sketch = lax.dynamic_slice_in_dim(
        sketch_cols, lax.axis_index(INNER) * block, block, 0
    )
    chunks = [own]
    for u, d in zip(ups, downs):
        chunks += [u, d]
    part, pair, pivot = pl.pallas_call(
        forward_body,
        in_specs=[SMEM] + [WHOLE] * 14,
        out_shape=(
            jax.ShapeDtypeStruct((rows, width), LOW),
            jax.ShapeDtypeStruct((slots, 128, width), FULL),
            jax.ShapeDtypeStruct((rows, slots * 128), LOW),
        ),
        scratch_shapes=[pltpu.VMEM((rows, slots * 128), LOW)],
        name="forward",
    )(place, *chunks, col_right, probe, all_left, target_right, own_sketch)
    pieces = lax.all_to_all(part.reshape(n, block, width), INNER, 0, 0, tiled=True)
    own_sum = jnp.sum(pieces.astype(FULL), 0)
    whole = to_all(own_sum.astype(LOW)).reshape(rows, width)
    basis, term, direct = pl.pallas_call(
        backward_body,
        in_specs=[SMEM] + [WHOLE] * 7,
        out_shape=(
            jax.ShapeDtypeStruct((block, width), FULL),
            jax.ShapeDtypeStruct((rows, width), LOW),
            jax.ShapeDtypeStruct((block, width), FULL),
        ),
        name="backward",
    )(place, whole, own_sum, pivot, pair, col_left, all_left, target_right)
    pieces = lax.all_to_all(term.reshape(n, block, width), INNER, 0, 0, tiled=True)
    coeffs = (jnp.sum(pieces.astype(FULL), 0) + direct) / rows
    return basis, coeffs


def solution(mesh):
    finer = Mesh(
        mesh.devices.reshape(mesh.shape["grp"], 8, 4, 2), ("grp", "inner_0", "inner_1", "inner_2")
    )
    return jax.shard_map(
        shards,
        mesh=finer,
        in_specs=(
            P(INNER, "grp", None),
            P(INNER, "grp", None),
            P(INNER, None, "grp"),
            P(INNER, None, "grp"),
            P(None, "grp"),
            P(INNER, "grp"),
            P(INNER, "grp"),
            P(INNER),
        ),
        out_specs=(P(INNER, "grp"), P(INNER, "grp")),
        check_vma=False,
    )
```

```python
import jax
import jax.numpy as jnp
from jax import lax
from jax.experimental import pallas as pl
from jax.experimental.pallas import tpu as pltpu
from jax.sharding import Mesh
from jax.sharding import PartitionSpec as P

INNER = ("inner_0", "inner_1", "inner_2")
LOW = jnp.bfloat16
FULL = jnp.float32


def dot(a, b, ca, cb):
    return lax.dot_general(a, b, (((ca,), (cb,)), ((), ())), preferred_element_type=FULL)


def halves(x):
    high = x.astype(LOW)
    return high, (x - high.astype(FULL)).astype(LOW)


def fine_dot(a, b, ca, cb):
    ah, al = halves(a)
    bh, bl = halves(b)
    return dot(ah, bh, ca, cb) + (dot(ah, bl, ca, cb) + dot(al, bh, ca, cb))


def spread(x, i):
    return jnp.broadcast_to(x[i : i + 1, :], x.shape)


def inverse_factors(grams):
    n, panel = grams[0].shape[0], 4
    count, groups = len(grams), n // 8
    sub = lax.broadcasted_iota(jnp.int32, (8, n), 0)
    lane = lax.broadcasted_iota(jnp.int32, (8, n), 1)
    left = [[g[8 * i : 8 * i + 8] for i in range(groups)] for g in grams]
    right = [[(lane == sub + 8 * i).astype(FULL) for i in range(groups)] for _ in grams]
    upper, lower = [[] for _ in grams], [[] for _ in grams]
    for p in range(groups):
        end = (p // panel + 1) * panel
        raw = [[[None] * 8 for _ in range(p, end)] for _ in grams]
        for some in (range(p, p + 1), range(p + 1, end)):
            for k in range(8):
                for t in range(count):
                    for g in some:
                        column = left[t][g][:, 8 * p + k : 8 * p + k + 1]
                        raw[t][g - p][k] = jnp.broadcast_to(column, (8, n))
        for t in range(count):
            a, b, col, pivots = left[t][p], right[t][p], list(raw[t][0]), None
            for k in range(8):
                pivot = spread(col[k], k)
                pivots = pivot if pivots is None else jnp.where(sub == k, pivot, pivots)
                if k < 7:
                    f = jnp.where(sub > k, col[k], 0.0) * (1.0 / pivot)
                    for i in range(k + 1, 8):
                        col[i] = col[i] - f * spread(col[i], k)
                    a, b = a - f * spread(a, k), b - f * spread(b, k)
            root = lax.rsqrt(pivots)
            upper[t].append(a * root)
            lower[t].append(b * root)
            if p + 1 < end:
                ratio = 1.0 / pivots
                y, z = a * ratio, b * ratio
                for i in range(7, 0, -1):
                    f = jnp.where(sub < i, col[i] * ratio, 0.0)
                    y, z = y - f * spread(y, i), z - f * spread(z, i)
                for g in range(p + 1, end):
                    for k in range(8):
                        c = raw[t][g - p][k]
                        left[t][g] = left[t][g] - c * spread(y, k)
                        right[t][g] = right[t][g] - c * spread(z, k)
        if p + 1 == end and end < groups:
            for t in range(count):
                ah, al = halves(jnp.concatenate(upper[t][end - panel :], 0))
                bh, bl = halves(jnp.concatenate(lower[t][end - panel :], 0))
                factor = jnp.concatenate([ah, ah, al], 0)
                cut_a = dot(factor, jnp.concatenate([ah, al, ah], 0), 0, 0)
                cut_b = dot(factor, jnp.concatenate([bh, bl, bh], 0), 0, 0)
                for g in range(end, groups):
                    left[t][g] = left[t][g] - cut_a[8 * g : 8 * g + 8]
                    right[t][g] = right[t][g] - cut_b[8 * g : 8 * g + 8]
    return [jnp.concatenate(rows, 0) for rows in lower]


def probe_body(left_ref, sketch_ref, out_ref):
    for k in range(left_ref.shape[0]):
        for t in range(out_ref.shape[1]):
            cols = slice(128 * t, 128 * t + 128)
            out_ref[k, t] = dot(left_ref[k, :, cols], sketch_ref[:, cols], 0, 0)


def early_body(place_ref, own, f1, b1, f2, b2, f3, b3, right_ref, pair_ref, pivot_ref, factor):
    group, groups = place_ref[0], place_ref[2]
    slots, n = right_ref.shape[0], own.shape[1]

    def put(ref, distance):
        at = pl.multiple_of(lax.rem(group + distance, groups) * n, n)
        for k in range(slots):
            cols = slice(128 * k, 128 * k + 128)
            if ref is None:
                factor[pl.ds(at, n), cols] = jnp.zeros((n, 128), LOW)
                pivot_ref[pl.ds(at, n), cols] = jnp.zeros((n, 128), LOW)
            else:
                factor[pl.ds(at, n), cols] = ref[k]
                pivot_ref[pl.ds(at, n), cols] = ref[k + slots]

    put(own, 0)
    for s, (f, b) in enumerate(((f1, b1), (f2, b2), (f3, b3))):
        put(f, groups - 1 - s)
        put(b, 1 + s)
    put(None, groups // 2)
    for k in range(slots):
        pair_ref[k] = dot(factor[:, 128 * k : 128 * k + 128], right_ref[k], 0, 0)


def forward_body(
    place_ref, f4, b4, early_ref, pivot_ref, right_ref, probe_ref, tall_ref, tright_ref,
    sketch_ref, keep_ref, send_ref, pair_ref, part,
):
    group, live, groups, core = place_ref[0], place_ref[1], place_ref[2], place_ref[3]
    slots, n, half = right_ref.shape[0], f4.shape[1], keep_ref.shape[0]
    at = pl.multiple_of(lax.rem(group + groups // 2, groups) * n, n)
    mixed = []
    for k in range(slots):
        pair = early_ref[k] + dot(f4[k], right_ref[k], 0, 0)
        pair_ref[k] = pair
        row = []
        for t in range(2):
            cols = slice(128 * t, 128 * t + 128)
            value = fine_dot(pair[:, cols], probe_ref[k, t], 1, 0)
            row.append(jnp.where(k < live, -value, 0.0).astype(LOW))
        mixed.append(jnp.concatenate(row, 1))
    mixed = jnp.concatenate(mixed, 0)
    update = dot(pivot_ref[...], mixed, 1, 0)
    for t in range(2):
        cols = slice(128 * t, 128 * t + 128)
        core_part = dot(tright_ref[:, cols], sketch_ref[:, cols], 0, 0).astype(LOW)
        part[:, cols] = update[:, cols] + dot(tall_ref[:, cols], core_part, 1, 0)
    last = jnp.concatenate([b4[k] for k in range(slots)], 1)
    part[pl.ds(at, n), :] += dot(last, mixed, 1, 0)
    whole = part[...].reshape(half, 2, 16, part.shape[1])
    keep_ref[...] = jnp.where(core == 0, whole[:, 0], whole[:, 1])
    send_ref[...] = jnp.where(core == 0, whole[:, 1], whole[:, 0])


def backward_body(
    place_ref, mine_ref, other_ref, own_ref, tright_ref, b4,
    pivot_any, pair_any, left_any, tall_any,
    basis_ref, term_ref, direct_ref,
    whole, pivot_ref, pair_ref, left_ref, tall_ref, sems,
):
    group, live, groups, core = place_ref[0], place_ref[1], place_ref[2], place_ref[3]
    copies = [
        pltpu.make_async_copy(source, target, sems.at[i])
        for i, (source, target) in enumerate(
            ((pivot_any, pivot_ref), (tall_any, tall_ref), (pair_any, pair_ref), (left_any, left_ref))
        )
    ]
    for c in copies:
        c.start()
    slots, rows, n = left_ref.shape[0], whole.shape[0], b4.shape[1]
    mine, other = mine_ref[...], other_ref[...]
    even, odd = jnp.where(core == 0, mine, other), jnp.where(core == 0, other, mine)
    whole[...] = jnp.concatenate([even[:, None], odd[:, None]], 1).reshape(rows, whole.shape[1])
    turned, grams = [], []
    for t in range(2):
        s = whole[:, 128 * t : 128 * t + 128]
        turned.append(s.T)
        grams.append(dot(turned[t], s, 1, 0) / rows)
    for c in copies:
        c.wait()
    at = pl.multiple_of(lax.rem(group + groups // 2, groups) * n, n)
    last = jnp.concatenate([b4[k] for k in range(slots)], 1)
    seen, seen_target = [], []
    for t in range(2):
        cols = slice(128 * t, 128 * t + 128)
        seen.append(
            dot(turned[t], pivot_ref[...], 1, 0) + dot(whole[pl.ds(at, n), cols], last, 0, 0)
        )
        seen_target.append(dot(turned[t], tall_ref[:, cols], 1, 0))
    inverse = inverse_factors(grams)
    for t in range(2):
        cols = slice(128 * t, 128 * t + 128)
        basis_ref[:, cols] = fine_dot(own_ref[:, cols], inverse[t], 1, 1)
        back = fine_dot(inverse[t], seen[t], 1, 0)
        total = None
        for k in range(slots):
            folded = fine_dot(back[:, 128 * k : 128 * k + 128], pair_ref[k, :, cols], 1, 0)
            folded = jnp.where(k < live, -folded, 0.0).astype(LOW)
            term = dot(left_ref[k, :, cols], folded, 1, 1)
            total = term if total is None else total + term
        term_ref[:, cols] = total.astype(LOW)
        target_back = fine_dot(inverse[t], seen_target[t], 1, 0).astype(LOW)
        direct_ref[:, cols] = dot(tright_ref[:, cols], target_back, 1, 1)


SMEM = pl.BlockSpec(memory_space=pltpu.SMEM)
WHOLE = pl.BlockSpec()
PLACED = pl.BlockSpec(memory_space=pl.ANY)


def shift(x, axis, by):
    n = lax.axis_size(axis)
    return lax.ppermute(x, axis, [(i, (i + by) % n) for i in range(n)])


def to_all(x, axes):
    n = lax.axis_size(axes)
    return lax.all_to_all(jnp.broadcast_to(x[None], (n, *x.shape)), axes, 0, 0, tiled=True)


def whole_block(x):
    return pl.BlockSpec(x.shape, lambda i, place: (0,) * x.ndim)


def shards(
    row_left, row_right, col_left, col_right, sketch_cols, target_left, target_right, live_counts
):
    slots, rows, width = col_left.shape
    block = target_left.shape[0]
    groups, chunk = lax.axis_size("grp"), row_left.shape[1]
    n, far = lax.axis_size(INNER), INNER[:2]
    place = jnp.stack(
        [lax.axis_index("grp"), live_counts[0], jnp.int32(groups), lax.axis_index(INNER[2])]
    ).astype(jnp.int32)
    own = jnp.concatenate([row_right, row_left], 0)
    chunks, up, down = [own], own, own
    for step in range(3):
        up, down = shift(up, "grp", 1), shift(down, "grp", -1)
        if step == 0:
            up, down, target_left = lax.optimization_barrier((up, down, target_left))
            all_left = to_all(target_left, INNER).reshape(rows, width)
            probe = pl.pallas_call(
                probe_body,
                out_shape=jax.ShapeDtypeStruct((slots, 2, 128, 128), FULL),
                name="probe",
            )(col_left, sketch_cols)
            own_sketch = lax.dynamic_slice_in_dim(
                sketch_cols, lax.axis_index(INNER) * block, block, 0
            )
        if step == 1:
            up, down, probe, own_sketch, place = lax.optimization_barrier(
                (up, down, probe, own_sketch, place)
            )
        chunks += [up, down]
    last_up, last_down = shift(up[:slots], "grp", 1), shift(down[slots:], "grp", -1)
    early, pivot = pl.pallas_call(
        early_body,
        in_specs=[SMEM] + [WHOLE] * 8,
        out_shape=(
            jax.ShapeDtypeStruct((slots, 128, width), FULL),
            jax.ShapeDtypeStruct((rows, slots * 128), LOW),
        ),
        scratch_shapes=[pltpu.VMEM((rows, slots * 128), LOW)],
        name="early",
    )(place, *chunks, col_right)
    ins = (last_up, last_down, early, pivot, col_right, probe, all_left, target_right, own_sketch)
    specs = [whole_block(x) for x in ins]
    specs[4] = pl.BlockSpec(
        (slots, chunk, width),
        lambda i, place: (0, lax.rem(place[0] + place[2] // 2, place[2]), 0),
    )
    outs = (
        jax.ShapeDtypeStruct((n // 2, block, width), FULL),
        jax.ShapeDtypeStruct((n // 2, block, width), FULL),
        jax.ShapeDtypeStruct((slots, 128, width), FULL),
    )
    keep, send, pair = pl.pallas_call(
        forward_body,
        grid_spec=pltpu.PrefetchScalarGridSpec(
            num_scalar_prefetch=1,
            grid=(1,),
            in_specs=specs,
            out_specs=[whole_block(x) for x in outs],
            scratch_shapes=[pltpu.VMEM((rows, width), FULL)],
        ),
        out_shape=outs,
        name="forward",
    )(place, *ins)
    summed = keep + shift(send, INNER[2], 1)
    own_sum = jnp.sum(lax.all_to_all(summed, far, 0, 0, tiled=True), 0)
    mine = to_all(own_sum.astype(LOW), far)
    other = shift(mine, INNER[2], 1)
    basis, term, direct = pl.pallas_call(
        backward_body,
        in_specs=[SMEM] + [WHOLE] * 5 + [PLACED] * 4,
        out_shape=(
            jax.ShapeDtypeStruct((block, width), FULL),
            jax.ShapeDtypeStruct((rows, width), LOW),
            jax.ShapeDtypeStruct((block, width), FULL),
        ),
        scratch_shapes=[
            pltpu.VMEM((rows, width), LOW),
            pltpu.VMEM(pivot.shape, LOW),
            pltpu.VMEM(pair.shape, FULL),
            pltpu.VMEM(col_left.shape, LOW),
            pltpu.VMEM(all_left.shape, LOW),
            pltpu.SemaphoreType.DMA((4,)),
        ],
        name="backward",
    )(place, mine, other, own_sum, target_right, last_down, pivot, pair, col_left, all_left)
    pieces = lax.all_to_all(term.reshape(n, block, width), INNER, 0, 0, tiled=True)
    coeffs = (jnp.sum(pieces.astype(FULL), 0) + direct) / rows
    return basis, coeffs


def solution(mesh):
    finer = Mesh(
        mesh.devices.reshape(mesh.shape["grp"], 8, 4, 2), ("grp", "inner_0", "inner_1", "inner_2")
    )
    return jax.shard_map(
        shards,
        mesh=finer,
        in_specs=(
            P(INNER, "grp", None),
            P(INNER, "grp", None),
            P(INNER, None, "grp"),
            P(INNER, None, "grp"),
            P(None, "grp"),
            P(INNER, "grp"),
            P(INNER, "grp"),
            P(INNER),
        ),
        out_specs=(P(INNER, "grp"), P(INNER, "grp")),
        check_vma=False,
    )
```

```python
import jax
import jax.numpy as jnp
from jax import lax
from jax.experimental import pallas as pl
from jax.experimental.pallas import tpu as pltpu
from jax.sharding import Mesh
from jax.sharding import PartitionSpec as P

INNER = ("inner_0", "inner_1", "inner_2")
LOW = jnp.bfloat16
FULL = jnp.float32


def dot(a, b, ca, cb):
    return lax.dot_general(a, b, (((ca,), (cb,)), ((), ())), preferred_element_type=FULL)


def halves(x):
    high = x.astype(LOW)
    return high, (x - high.astype(FULL)).astype(LOW)


def fine_dot(a, b, ca, cb):
    ah, al = halves(a)
    bh, bl = halves(b)
    return dot(ah, bh, ca, cb) + (dot(ah, bl, ca, cb) + dot(al, bh, ca, cb))


def spread(x, i):
    return jnp.broadcast_to(x[i : i + 1, :], x.shape)


def inverse_factors(grams):
    n, panel = grams[0].shape[0], 4
    count, groups = len(grams), n // 8
    sub = lax.broadcasted_iota(jnp.int32, (8, n), 0)
    lane = lax.broadcasted_iota(jnp.int32, (8, n), 1)
    left = [[g[8 * i : 8 * i + 8] for i in range(groups)] for g in grams]
    right = [[(lane == sub + 8 * i).astype(FULL) for i in range(groups)] for _ in grams]
    upper, lower = [[] for _ in grams], [[] for _ in grams]
    for p in range(groups):
        end = (p // panel + 1) * panel
        raw = [[[None] * 8 for _ in range(p, end)] for _ in grams]
        for some in (range(p, p + 1), range(p + 1, end)):
            for k in range(8):
                for t in range(count):
                    for g in some:
                        column = left[t][g][:, 8 * p + k : 8 * p + k + 1]
                        raw[t][g - p][k] = jnp.broadcast_to(column, (8, n))
        for t in range(count):
            a, b, col, pivots = left[t][p], right[t][p], list(raw[t][0]), None
            for k in range(8):
                pivot = spread(col[k], k)
                pivots = pivot if pivots is None else jnp.where(sub == k, pivot, pivots)
                if k < 7:
                    f = jnp.where(sub > k, col[k], 0.0) * (1.0 / pivot)
                    for i in range(k + 1, 8):
                        col[i] = col[i] - f * spread(col[i], k)
                    a, b = a - f * spread(a, k), b - f * spread(b, k)
            root = lax.rsqrt(pivots)
            upper[t].append(a * root)
            lower[t].append(b * root)
            if p + 1 < end:
                ratio = 1.0 / pivots
                y, z = a * ratio, b * ratio
                for i in range(7, 0, -1):
                    f = jnp.where(sub < i, col[i] * ratio, 0.0)
                    y, z = y - f * spread(y, i), z - f * spread(z, i)
                for g in range(p + 1, end):
                    for k in range(8):
                        c = raw[t][g - p][k]
                        left[t][g] = left[t][g] - c * spread(y, k)
                        right[t][g] = right[t][g] - c * spread(z, k)
        if p + 1 == end and end < groups:
            for t in range(count):
                ah, al = halves(jnp.concatenate(upper[t][end - panel :], 0))
                bh, bl = halves(jnp.concatenate(lower[t][end - panel :], 0))
                factor = jnp.concatenate([ah, ah, al], 0)
                cut_a = dot(factor, jnp.concatenate([ah, al, ah], 0), 0, 0)
                cut_b = dot(factor, jnp.concatenate([bh, bl, bh], 0), 0, 0)
                for g in range(end, groups):
                    left[t][g] = left[t][g] - cut_a[8 * g : 8 * g + 8]
                    right[t][g] = right[t][g] - cut_b[8 * g : 8 * g + 8]
    return [jnp.concatenate(rows, 0) for rows in lower]


def probe_body(left_ref, sketch_ref, out_ref):
    for k in range(left_ref.shape[0]):
        for t in range(out_ref.shape[1]):
            cols = slice(128 * t, 128 * t + 128)
            out_ref[k, t] = dot(left_ref[k, :, cols], sketch_ref[:, cols], 0, 0)


def early_body(place_ref, own, f1, b1, f2, b2, f3, b3, right_ref, pair_ref, pivot_ref, factor):
    group, groups = place_ref[0], place_ref[2]
    slots, n = right_ref.shape[0], own.shape[1]

    def put(ref, distance):
        at = pl.multiple_of(lax.rem(group + distance, groups) * n, n)
        for k in range(slots):
            cols = slice(128 * k, 128 * k + 128)
            if ref is None:
                factor[pl.ds(at, n), cols] = jnp.zeros((n, 128), LOW)
                pivot_ref[pl.ds(at, n), cols] = jnp.zeros((n, 128), LOW)
            else:
                factor[pl.ds(at, n), cols] = ref[k]
                pivot_ref[pl.ds(at, n), cols] = ref[k + slots]

    put(own, 0)
    for s, (f, b) in enumerate(((f1, b1), (f2, b2), (f3, b3))):
        put(f, groups - 1 - s)
        put(b, 1 + s)
    put(None, groups // 2)
    for k in range(slots):
        pair_ref[k] = dot(factor[:, 128 * k : 128 * k + 128], right_ref[k], 0, 0)


def forward_body(
    place_ref, f4, b4, early_ref, pivot_ref, probe_ref, sketch_ref, right_ref, tright_ref,
    keep_ref, send_ref, pair_ref, core_ref, part,
):
    group, live, groups, core = place_ref[0], place_ref[1], place_ref[2], place_ref[3]
    slots, n, half = right_ref.shape[0], f4.shape[1], keep_ref.shape[0]
    at = pl.multiple_of(lax.rem(group + groups // 2, groups) * n, n)
    mixed = []
    for k in range(slots):
        pair = early_ref[k] + dot(f4[k], right_ref[k, pl.ds(at, n), :], 0, 0)
        pair_ref[k] = pair
        row = []
        for t in range(2):
            cols = slice(128 * t, 128 * t + 128)
            value = fine_dot(pair[:, cols], probe_ref[k, t], 1, 0)
            row.append(jnp.where(k < live, -value, 0.0).astype(LOW))
        mixed.append(jnp.concatenate(row, 1))
    mixed = jnp.concatenate(mixed, 0)
    part[...] = dot(pivot_ref[...], mixed, 1, 0)
    last = jnp.concatenate([b4[k] for k in range(slots)], 1)
    part[pl.ds(at, n), :] = dot(last, mixed, 1, 0)
    cores = [
        dot(tright_ref[:, 128 * t : 128 * t + 128], sketch_ref[:, 128 * t : 128 * t + 128], 0, 0)
        for t in range(2)
    ]
    core_ref[...] = jnp.concatenate(halves(jnp.concatenate(cores, 0).reshape(half, 8, 128)), 1)
    whole = part[...].reshape(half, 2, 16, part.shape[1])
    keep_ref[...] = jnp.where(core == 0, whole[:, 0], whole[:, 1])
    send_ref[...] = jnp.where(core == 0, whole[:, 1], whole[:, 0])


def merge_body(keep_ref, come_ref, core_ref, out_ref):
    width = keep_ref.shape[2]
    out_ref[:, :, :width] = (keep_ref[...] + come_ref[...]).astype(LOW)
    out_ref[:, :, width:] = core_ref[...]


def own_body(pieces_ref, tleft_ref, sum_ref, out_ref):
    width = sum_ref.shape[1]
    total = jnp.sum(pieces_ref[...].astype(FULL), 0)
    sum_ref[...] = total[:, :width]
    core = jnp.concatenate(halves(total[:8, width:] + total[8:, width:]), 0)
    row = jnp.concatenate([total[:, :width].astype(LOW), tleft_ref[...], core], 1)
    out_ref[...] = jnp.broadcast_to(row[None], out_ref.shape)


def backward_body(
    place_ref, mine_ref, other_ref, own_ref, b4, pivot_ref, pair_ref, tleft_ref, tright_ref,
    left_ref, basis_ref, term_ref, direct_ref, turn_high, turn_low, tall,
):
    group, live, groups, core = place_ref[0], place_ref[1], place_ref[2], place_ref[3]
    slots, rows, n = left_ref.shape[0], tall.shape[0], b4.shape[1]
    width = own_ref.shape[1]

    def ordered(cols):
        mine, other = mine_ref[:, :, cols], other_ref[:, :, cols]
        even, odd = jnp.where(core == 0, mine, other), jnp.where(core == 0, other, mine)
        return jnp.concatenate([even[:, None], odd[:, None]], 1).reshape(rows, -1)

    tall[...] = ordered(slice(width, 2 * width))
    parts = mine_ref[:, :, 2 * width :].astype(FULL) + other_ref[:, :, 2 * width :].astype(FULL)
    cores = (parts[:, :8] + parts[:, 8:]).reshape(2 * 128, 128).astype(LOW)
    at = pl.multiple_of(lax.rem(group + groups // 2, groups) * n, n)
    last = jnp.concatenate([b4[k] for k in range(slots)], 1)
    whole, own, grams, seen, seen_target = [], [], [], [], []
    for t in range(2):
        cols = slice(128 * t, 128 * t + 128)
        target_core = cores[cols]
        s = ordered(cols).astype(FULL) + dot(tall[:, cols], target_core, 1, 0)
        own.append(own_ref[:, cols] + dot(tleft_ref[:, cols], target_core, 1, 0))
        turned = s.T
        high, low = halves(turned)
        grams.append(dot(high, s.astype(LOW), 1, 0) / rows)
        turn_high[t] = high
        turn_low[t] = low
    for t in range(2):
        cols = slice(128 * t, 128 * t + 128)
        both = jnp.concatenate([turn_high[t], turn_low[t]], 0)
        product = dot(both, pivot_ref[...], 1, 0)
        tail = jnp.concatenate([turn_high[t, :, pl.ds(at, n)], turn_low[t, :, pl.ds(at, n)]], 0)
        product = product + dot(tail, last, 1, 0)
        seen.append(product[:128] + product[128:])
        product = dot(both, tall[:, cols], 1, 0)
        seen_target.append(product[:128] + product[128:])
    inverse = inverse_factors(grams)
    for t in range(2):
        cols = slice(128 * t, 128 * t + 128)
        basis_ref[:, cols] = fine_dot(own[t], inverse[t], 1, 1)
        back = fine_dot(inverse[t], seen[t], 1, 0)
        total = None
        for k in range(slots):
            folded = fine_dot(back[:, 128 * k : 128 * k + 128], pair_ref[k, :, cols], 1, 0)
            folded = jnp.where(k < live, -folded, 0.0).astype(LOW)
            term = dot(left_ref[k, :, cols], folded, 1, 1)
            total = term if total is None else total + term
        term_ref[:, cols] = total.astype(LOW)
        target_back = fine_dot(inverse[t], seen_target[t], 1, 0).astype(LOW)
        direct_ref[:, cols] = dot(tright_ref[:, cols], target_back, 1, 1)


SMEM = pl.BlockSpec(memory_space=pltpu.SMEM)
VMEM = pl.BlockSpec(memory_space=pltpu.VMEM)


def shift(x, axis, by):
    n = lax.axis_size(axis)
    return lax.ppermute(x, axis, [(i, (i + by) % n) for i in range(n)])


def near(x):
    return pltpu.with_memory_space_constraint(x, pltpu.VMEM)


def kernel(body, name, outs, scratch, place, *arrays, given=()):
    first = () if place is None else (place,)
    return pl.pallas_call(
        body,
        in_specs=[SMEM] * len(first) + [VMEM] * (len(arrays) + len(given)),
        out_specs=[VMEM] * len(outs),
        out_shape=[pltpu.VMEM(*o) for o in outs],
        scratch_shapes=[pltpu.VMEM(*o) for o in scratch],
        name=name,
        compiler_params=pltpu.CompilerParams(vmem_limit_bytes=24 << 20),
    )(*first, *[near(x) for x in arrays], *given)


def shards(
    row_left, row_right, col_left, col_right, sketch_cols, target_left, target_right, live_counts
):
    slots, rows, width = col_left.shape
    block, factors = target_left.shape[0], slots * 128
    n, far, groups = lax.axis_size(INNER), INNER[:2], lax.axis_size("grp")
    half = n // 2
    place = jnp.stack(
        [lax.axis_index("grp"), live_counts[0], jnp.int32(groups), lax.axis_index(INNER[2])]
    ).astype(jnp.int32)
    own = jnp.concatenate([row_right, row_left], 0)
    chunks, up, down = [own], own, own
    for step in range(3):
        up, down = shift(up, "grp", 1), shift(down, "grp", -1)
        if step == 0:
            (probe,) = kernel(
                probe_body,
                "probe",
                [((slots, 2, 128, 128), FULL)],
                [],
                None,
                given=(col_left, sketch_cols),
            )
            own_sketch = lax.dynamic_slice_in_dim(
                sketch_cols, lax.axis_index(INNER) * block, block, 0
            )
        if step == 1:
            up, down, probe, own_sketch, place = lax.optimization_barrier(
                (up, down, probe, own_sketch, place)
            )
        chunks += [up, down]
    last_up, last_down = shift(up[:slots], "grp", 1), shift(down[slots:], "grp", -1)
    early, pivot = kernel(
        early_body,
        "early",
        [((slots, 128, width), FULL), ((rows, factors), LOW)],
        [((rows, factors), LOW)],
        place,
        *chunks,
        given=(col_right,),
    )
    piece = (half, block, width)
    keep, send, pair, core = kernel(
        forward_body,
        "forward",
        [(piece, FULL), (piece, FULL), ((slots, 128, width), FULL), ((half, block, 128), LOW)],
        [((rows, width), FULL)],
        place,
        last_up,
        last_down,
        early,
        pivot,
        probe,
        own_sketch,
        given=(col_right, target_right),
    )
    (merged,) = kernel(
        merge_body, "merge", [((half, block, width + 128), LOW)], [], None,
        keep, shift(send, INNER[2], 1), core,
    )
    own_sum, mine = kernel(
        own_body,
        "own",
        [((block, width), FULL), ((half, block, 2 * width + 128), LOW)],
        [],
        None,
        lax.all_to_all(merged, far, 0, 0, tiled=True),
        given=(target_left,),
    )
    mine = lax.all_to_all(mine, far, 0, 0, tiled=True)
    other = shift(mine, INNER[2], 1)
    basis, term, direct = kernel(
        backward_body,
        "backward",
        [((block, width), FULL), ((rows, width), LOW), ((block, width), FULL)],
        [((2, 128, rows), LOW), ((2, 128, rows), LOW), ((rows, width), LOW)],
        place,
        mine,
        other,
        own_sum,
        last_down,
        pivot,
        pair,
        given=(target_left, target_right, col_left),
    )
    pieces = lax.all_to_all(term.reshape(n, block, width), INNER, 0, 0, tiled=True)
    coeffs = (jnp.sum(pieces.astype(FULL), 0) + direct) / rows
    return basis, coeffs


def solution(mesh):
    finer = Mesh(
        mesh.devices.reshape(mesh.shape["grp"], 8, 4, 2), ("grp", "inner_0", "inner_1", "inner_2")
    )
    return jax.shard_map(
        shards,
        mesh=finer,
        in_specs=(
            P(INNER, "grp", None),
            P(INNER, "grp", None),
            P(INNER, None, "grp"),
            P(INNER, None, "grp"),
            P(None, "grp"),
            P(INNER, "grp"),
            P(INNER, "grp"),
            P(INNER),
        ),
        out_specs=(P(INNER, "grp"), P(INNER, "grp")),
        check_vma=False,
    )
```

```python
import functools

import jax
import jax.numpy as jnp
from jax import lax
from jax.experimental import pallas as pl
from jax.experimental.pallas import tpu as pltpu
from jax.sharding import Mesh
from jax.sharding import PartitionSpec as P

INNER = ("inner_0", "inner_1", "inner_2")
LOW = jnp.bfloat16
FULL = jnp.float32


def dot(a, b, ca, cb):
    return lax.dot_general(a, b, (((ca,), (cb,)), ((), ())), preferred_element_type=FULL)


def halves(x):
    high = x.astype(LOW)
    return high, (x - high.astype(FULL)).astype(LOW)


def fine_dot(a, b, ca, cb):
    ah, al = halves(a)
    bh, bl = halves(b)
    return dot(ah, bh, ca, cb) + (dot(ah, bl, ca, cb) + dot(al, bh, ca, cb))


def spread(x, i):
    return jnp.broadcast_to(x[i : i + 1, :], x.shape)


def inverse_factors(grams):
    n, panel = grams[0].shape[0], 4
    count, groups = len(grams), n // 8
    sub = lax.broadcasted_iota(jnp.int32, (8, n), 0)
    lane = lax.broadcasted_iota(jnp.int32, (8, n), 1)
    left = [[g[8 * i : 8 * i + 8] for i in range(groups)] for g in grams]
    right = [[(lane == sub + 8 * i).astype(FULL) for i in range(groups)] for _ in grams]
    upper, lower = [[] for _ in grams], [[] for _ in grams]
    for p in range(groups):
        end = (p // panel + 1) * panel
        raw = [[[None] * 8 for _ in range(p, end)] for _ in grams]
        for some in (range(p, p + 1), range(p + 1, end)):
            for k in range(8):
                for t in range(count):
                    for g in some:
                        column = left[t][g][:, 8 * p + k : 8 * p + k + 1]
                        raw[t][g - p][k] = jnp.broadcast_to(column, (8, n))
        for t in range(count):
            a, b, col, pivots = left[t][p], right[t][p], list(raw[t][0]), None
            for k in range(8):
                pivot = spread(col[k], k)
                pivots = pivot if pivots is None else jnp.where(sub == k, pivot, pivots)
                if k < 7:
                    f = jnp.where(sub > k, col[k], 0.0) * (1.0 / pivot)
                    for i in range(k + 1, 8):
                        col[i] = col[i] - f * spread(col[i], k)
                    a, b = a - f * spread(a, k), b - f * spread(b, k)
            root = lax.rsqrt(pivots)
            upper[t].append(a * root)
            lower[t].append(b * root)
            if p + 1 < end:
                ratio = 1.0 / pivots
                y, z = a * ratio, b * ratio
                for i in range(7, 0, -1):
                    f = jnp.where(sub < i, col[i] * ratio, 0.0)
                    y, z = y - f * spread(y, i), z - f * spread(z, i)
                for g in range(p + 1, end):
                    for k in range(8):
                        c = raw[t][g - p][k]
                        left[t][g] = left[t][g] - c * spread(y, k)
                        right[t][g] = right[t][g] - c * spread(z, k)
        if p + 1 == end and end < groups:
            for t in range(count):
                ah, al = halves(jnp.concatenate(upper[t][end - panel :], 0))
                bh, bl = halves(jnp.concatenate(lower[t][end - panel :], 0))
                factor = jnp.concatenate([ah, ah, al], 0)
                cut_a = dot(factor, jnp.concatenate([ah, al, ah], 0), 0, 0)
                cut_b = dot(factor, jnp.concatenate([bh, bl, bh], 0), 0, 0)
                for g in range(end, groups):
                    left[t][g] = left[t][g] - cut_a[8 * g : 8 * g + 8]
                    right[t][g] = right[t][g] - cut_b[8 * g : 8 * g + 8]
    return [jnp.concatenate(rows, 0) for rows in lower]


def join_body(right_any, left_any, out_ref, sems):
    slots = right_any.shape[0]
    copies = [
        pltpu.make_async_copy(right_any, out_ref.at[:slots], sems.at[0]),
        pltpu.make_async_copy(left_any, out_ref.at[slots:], sems.at[1]),
    ]
    for c in copies:
        c.start()
    for c in copies:
        c.wait()


def probe_body(left_any, sketch_any, out_ref, left_ref, sketch_ref, sems, *, first):
    count = out_ref.shape[0]
    copies = [pltpu.make_async_copy(sketch_any, sketch_ref, sems.at[count])]
    for k in range(count):
        copies.append(
            pltpu.make_async_copy(left_any.at[first + k], left_ref.at[k], sems.at[k])
        )
    for c in copies:
        c.start()
    copies[0].wait()
    for k in range(count):
        copies[1 + k].wait()
        for t in range(2):
            cols = slice(128 * t, 128 * t + 128)
            out_ref[k, t] = dot(left_ref[k, :, cols], sketch_ref[:, cols], 0, 0)


def early_body(place_ref, own, f1, b1, f2, b2, f3, b3, right_ref, pair_ref, pivot_ref, factor):
    group, groups, core = place_ref[0], place_ref[2], place_ref[3]
    slots, n = right_ref.shape[0], own.shape[1]

    def put(ref, distance):
        at = pl.multiple_of(lax.rem(group + distance, groups) * n, n)
        for k in range(slots):
            cols = slice(128 * k, 128 * k + 128)
            if ref is None:
                factor[pl.ds(at, n), cols] = jnp.zeros((n, 128), LOW)
                pivot_ref[pl.ds(at, n), cols] = jnp.zeros((n, 128), LOW)
            else:
                factor[pl.ds(at, n), cols] = ref[k]
                pivot_ref[pl.ds(at, n), cols] = ref[k + slots]

    put(own, 0)
    for s, (f, b) in enumerate(((f1, b1), (f2, b2), (f3, b3))):
        put(f, jnp.where(core == 0, groups - 1 - s, 1 + s))
        put(b, jnp.where(core == 0, 1 + s, groups - 1 - s))
    put(None, groups // 2)
    for k in range(slots):
        pair_ref[k] = dot(factor[:, 128 * k : 128 * k + 128], right_ref[k], 0, 0)


def forward_body(
    place_ref, f4, b4, early_ref, pivot_ref, probe_low, probe_high, sketch_ref, right_ref, tright_ref,
    keep_ref, send_ref, pair_ref, core_ref, part,
):
    group, live, groups, core = place_ref[0], place_ref[1], place_ref[2], place_ref[3]
    slots, n, half = right_ref.shape[0], f4.shape[1], keep_ref.shape[0]
    at = pl.multiple_of(lax.rem(group + groups // 2, groups) * n, n)
    mixed = []
    for k in range(slots):
        pair = early_ref[k] + dot(f4[k], right_ref[k, pl.ds(at, n), :], 0, 0)
        pair_ref[k] = pair
        row = []
        for t in range(2):
            cols = slice(128 * t, 128 * t + 128)
            probe = probe_low if k < probe_low.shape[0] else probe_high
            value = fine_dot(pair[:, cols], probe[k % probe_low.shape[0], t], 1, 0)
            row.append(jnp.where(k < live, -value, 0.0).astype(LOW))
        mixed.append(jnp.concatenate(row, 1))
    mixed = jnp.concatenate(mixed, 0)
    part[...] = dot(pivot_ref[...], mixed, 1, 0)
    last = jnp.concatenate([b4[k] for k in range(slots)], 1)
    part[pl.ds(at, n), :] = dot(last, mixed, 1, 0)
    cores = [
        dot(tright_ref[:, 128 * t : 128 * t + 128], sketch_ref[:, 128 * t : 128 * t + 128], 0, 0)
        for t in range(2)
    ]
    core_ref[...] = jnp.concatenate(halves(jnp.concatenate(cores, 0).reshape(half, 8, 128)), 1)
    whole = part[...].reshape(half, 2, 16, part.shape[1])
    keep_ref[...] = jnp.where(core == 0, whole[:, 0], whole[:, 1])
    send_ref[...] = jnp.where(core == 0, whole[:, 1], whole[:, 0])


def add_body(keep_ref, come_ref, out_ref):
    out_ref[...] = (keep_ref[...] + come_ref[...]).astype(LOW)


def last_body(pieces_ref, direct_ref, out_ref, *, rows):
    out_ref[...] = (jnp.sum(pieces_ref[...].astype(FULL), 0) + direct_ref[...]) / rows


def merge_body(keep_ref, come_ref, core_ref, out_ref):
    width = keep_ref.shape[2]
    out_ref[:, :, :width] = (keep_ref[...] + come_ref[...]).astype(LOW)
    out_ref[:, :, width:] = core_ref[...]


def own_body(pieces_ref, tleft_ref, sum_ref, out_ref):
    width = sum_ref.shape[1]
    total = jnp.sum(pieces_ref[...].astype(FULL), 0)
    sum_ref[...] = total[:, :width]
    core = jnp.concatenate(halves(total[:8, width:] + total[8:, width:]), 0)
    row = jnp.concatenate([total[:, :width].astype(LOW), tleft_ref[...], core], 1)
    out_ref[...] = jnp.broadcast_to(row[None], out_ref.shape)


def backward_body(
    place_ref, mine_ref, other_ref, own_ref, b4, pivot_ref, pair_ref, tleft_ref, tright_ref,
    left_ref, basis_ref, keep_ref, send_ref, direct_ref, turn_high, turn_low, tall,
):
    group, live, groups, core = place_ref[0], place_ref[1], place_ref[2], place_ref[3]
    slots, rows, n = left_ref.shape[0], tall.shape[0], b4.shape[1]
    width = own_ref.shape[1]

    def ordered(cols):
        mine, other = mine_ref[:, :, cols], other_ref[:, :, cols]
        even, odd = jnp.where(core == 0, mine, other), jnp.where(core == 0, other, mine)
        return jnp.concatenate([even[:, None], odd[:, None]], 1).reshape(rows, -1)

    tall[...] = ordered(slice(width, 2 * width))
    parts = mine_ref[:, :, 2 * width :].astype(FULL) + other_ref[:, :, 2 * width :].astype(FULL)
    cores = (parts[:, :8] + parts[:, 8:]).reshape(2 * 128, 128).astype(LOW)
    at = pl.multiple_of(lax.rem(group + groups // 2, groups) * n, n)
    last = jnp.concatenate([b4[k] for k in range(slots)], 1)
    whole, own, grams, seen, seen_target = [], [], [], [], []
    for t in range(2):
        cols = slice(128 * t, 128 * t + 128)
        target_core = cores[cols]
        s = ordered(cols).astype(FULL) + dot(tall[:, cols], target_core, 1, 0)
        own.append(own_ref[:, cols] + dot(tleft_ref[:, cols], target_core, 1, 0))
        turned = s.T
        high, low = halves(turned)
        grams.append(dot(high, s.astype(LOW), 1, 0) / rows)
        turn_high[t] = high
        turn_low[t] = low
    for t in range(2):
        cols = slice(128 * t, 128 * t + 128)
        both = jnp.concatenate([turn_high[t], turn_low[t]], 0)
        product = dot(both, pivot_ref[...], 1, 0)
        tail = jnp.concatenate([turn_high[t, :, pl.ds(at, n)], turn_low[t, :, pl.ds(at, n)]], 0)
        product = product + dot(tail, last, 1, 0)
        seen.append(product[:128] + product[128:])
        product = dot(both, tall[:, cols], 1, 0)
        seen_target.append(product[:128] + product[128:])
    inverse = inverse_factors(grams)
    for t in range(2):
        cols = slice(128 * t, 128 * t + 128)
        basis_ref[:, cols] = fine_dot(own[t], inverse[t], 1, 1)
        back = fine_dot(inverse[t], seen[t], 1, 0)
        total = None
        for k in range(slots):
            folded = fine_dot(back[:, 128 * k : 128 * k + 128], pair_ref[k, :, cols], 1, 0)
            folded = jnp.where(k < live, -folded, 0.0).astype(LOW)
            term = dot(left_ref[k, :, cols], folded, 1, 1)
            total = term if total is None else total + term
        total = total.reshape(keep_ref.shape[0], 2, 16, 128)
        keep_ref[:, :, cols] = jnp.where(core == 0, total[:, 0], total[:, 1])
        send_ref[:, :, cols] = jnp.where(core == 0, total[:, 1], total[:, 0])
        target_back = fine_dot(inverse[t], seen_target[t], 1, 0).astype(LOW)
        direct_ref[:, cols] = dot(tright_ref[:, cols], target_back, 1, 1)


SMEM = pl.BlockSpec(memory_space=pltpu.SMEM)
VMEM = pl.BlockSpec(memory_space=pltpu.VMEM)


def shift(x, axis, by):
    n = lax.axis_size(axis)
    return lax.ppermute(x, axis, [(i, (i + by) % n) for i in range(n)])


def around(x, by):
    n = lax.axis_size("grp")
    pairs = [
        (2 * i + core, 2 * ((i + (by if core == 0 else -by)) % n) + core)
        for i in range(n)
        for core in range(2)
    ]
    return lax.ppermute(x, ("grp", INNER[2]), pairs)


def near(x):
    return pltpu.with_memory_space_constraint(x, pltpu.VMEM)


def kernel(body, name, outs, scratch, place, *arrays, given=(), leave=None):
    first = () if place is None else (place,)
    return pl.pallas_call(
        body,
        in_specs=[SMEM] * len(first) + [VMEM] * (len(arrays) + len(given)),
        out_specs=[VMEM] * len(outs),
        out_shape=[
            (jax.ShapeDtypeStruct if o[0] == leave else pltpu.VMEM)(*o) for o in outs
        ],
        scratch_shapes=[pltpu.VMEM(*o) for o in scratch],
        name=name,
        compiler_params=pltpu.CompilerParams(vmem_limit_bytes=24 << 20),
    )(*first, *[near(x) for x in arrays], *given)


def probed(col_left, sketch_cols, first, count):
    return pl.pallas_call(
        functools.partial(probe_body, first=first),
        in_specs=[pl.BlockSpec(memory_space=pltpu.HBM)] * 2,
        out_specs=VMEM,
        out_shape=pltpu.VMEM((count, 2, 128, 128), FULL),
        scratch_shapes=[
            pltpu.VMEM((count, *col_left.shape[1:]), LOW),
            pltpu.VMEM(sketch_cols.shape, LOW),
            pltpu.SemaphoreType.DMA((count + 1,)),
        ],
        name="probe",
        compiler_params=pltpu.CompilerParams(vmem_limit_bytes=24 << 20),
    )(*(pltpu.with_memory_space_constraint(x, pltpu.HBM) for x in (col_left, sketch_cols)))


def shards(
    row_left, row_right, col_left, col_right, sketch_cols, target_left, target_right, live_counts
):
    slots, rows, width = col_left.shape
    block, factors = target_left.shape[0], slots * 128
    n, far, groups = lax.axis_size(INNER), INNER[:2], lax.axis_size("grp")
    half = n // 2
    place = jnp.stack(
        [lax.axis_index("grp"), live_counts[0], jnp.int32(groups), lax.axis_index(INNER[2])]
    ).astype(jnp.int32)
    own = pl.pallas_call(
        join_body,
        in_specs=[pl.BlockSpec(memory_space=pltpu.HBM)] * 2,
        out_specs=VMEM,
        out_shape=pltpu.VMEM((2 * slots, *row_left.shape[1:]), LOW),
        scratch_shapes=[pltpu.SemaphoreType.DMA((2,))],
        name="join",
        compiler_params=pltpu.CompilerParams(vmem_limit_bytes=24 << 20),
    )(*(pltpu.with_memory_space_constraint(x, pltpu.HBM) for x in (row_right, row_left)))
    chunks, probes, up, down = [own], [], own, own
    for step in range(3):
        up, down = around(up, 1), around(down, -1)
        if step == 0:
            own_sketch = lax.dynamic_slice_in_dim(
                sketch_cols, lax.axis_index(INNER) * block, block, 0
            )
        if step < 2:
            probe = probed(col_left, sketch_cols, step * (slots // 2), slots // 2)
            up, down, probe, own_sketch, place = lax.optimization_barrier(
                (up, down, probe, own_sketch, place)
            )
            probes.append(probe)
        chunks += [up, down]
    last_up, last_down = around(up[:slots], 1), around(down[slots:], -1)
    early, pivot = kernel(
        early_body,
        "early",
        [((slots, 128, width), FULL), ((rows, factors), LOW)],
        [((rows, factors), LOW)],
        place,
        *chunks,
        given=(col_right,),
    )
    piece = (half, block, width)
    keep, send, pair, core = kernel(
        forward_body,
        "forward",
        [(piece, FULL), (piece, FULL), ((slots, 128, width), FULL), ((half, block, 128), LOW)],
        [((rows, width), FULL)],
        place,
        last_up,
        last_down,
        early,
        pivot,
        *probes,
        own_sketch,
        given=(col_right, target_right),
    )
    (merged,) = kernel(
        merge_body, "merge", [((half, block, width + 128), LOW)], [], None,
        keep, shift(send, INNER[2], 1), core,
    )
    own_sum, mine = kernel(
        own_body,
        "own",
        [((block, width), FULL), ((half, block, 2 * width + 128), LOW)],
        [],
        None,
        lax.all_to_all(merged, far, 0, 0, tiled=True),
        given=(target_left,),
    )
    mine = lax.all_to_all(mine, far, 0, 0, tiled=True)
    other = shift(mine, INNER[2], 1)
    basis, keep, send, direct = kernel(
        backward_body,
        "backward",
        [((block, width), FULL), (piece, FULL), (piece, FULL), ((block, width), FULL)],
        [((2, 128, rows), LOW), ((2, 128, rows), LOW), ((rows, width), LOW)],
        place,
        mine,
        other,
        own_sum,
        last_down,
        pivot,
        pair,
        given=(target_left, target_right, col_left),
    )
    (merged,) = kernel(add_body, "add", [(piece, LOW)], [], None, keep, shift(send, INNER[2], 1))
    (coeffs,) = kernel(
        functools.partial(last_body, rows=rows),
        "last",
        [((block, width), FULL)],
        [],
        None,
        lax.all_to_all(merged, far, 0, 0, tiled=True),
        direct,
        leave=(block, width),
    )
    return basis, coeffs


def solution(mesh):
    finer = Mesh(
        mesh.devices.reshape(mesh.shape["grp"], 8, 4, 2), ("grp", "inner_0", "inner_1", "inner_2")
    )
    return jax.shard_map(
        shards,
        mesh=finer,
        in_specs=(
            P(INNER, "grp", None),
            P(INNER, "grp", None),
            P(INNER, None, "grp"),
            P(INNER, None, "grp"),
            P(None, "grp"),
            P(INNER, "grp"),
            P(INNER, "grp"),
            P(INNER),
        ),
        out_specs=(P(INNER, "grp"), P(INNER, "grp")),
        check_vma=False,
    )
```

```python
import functools

import jax
import jax.numpy as jnp
from jax import lax
from jax.experimental import pallas as pl
from jax.experimental.pallas import tpu as pltpu
from jax.sharding import Mesh
from jax.sharding import PartitionSpec as P

INNER = ("inner_0", "inner_1", "inner_2")
LOW = jnp.bfloat16
FULL = jnp.float32


def dot(a, b, ca, cb):
    return lax.dot_general(a, b, (((ca,), (cb,)), ((), ())), preferred_element_type=FULL)


def halves(x):
    high = x.astype(LOW)
    return high, (x - high.astype(FULL)).astype(LOW)


def fine_dot(a, b, ca, cb):
    ah, al = halves(a)
    bh, bl = halves(b)
    return dot(ah, bh, ca, cb) + (dot(ah, bl, ca, cb) + dot(al, bh, ca, cb))


def spread(x, i):
    return jnp.broadcast_to(x[i : i + 1, :], x.shape)


def inverse_factors(grams):
    n, panel = grams[0].shape[0], 4
    count, groups = len(grams), n // 8
    sub = lax.broadcasted_iota(jnp.int32, (8, n), 0)
    lane = lax.broadcasted_iota(jnp.int32, (8, n), 1)
    left = [[g[8 * i : 8 * i + 8] for i in range(groups)] for g in grams]
    right = [[(lane == sub + 8 * i).astype(FULL) for i in range(groups)] for _ in grams]
    upper, lower = [[] for _ in grams], [[] for _ in grams]
    for p in range(groups):
        end = (p // panel + 1) * panel
        raw = [[[None] * 8 for _ in range(p, end)] for _ in grams]
        for some in (range(p, p + 1), range(p + 1, end)):
            for k in range(8):
                for t in range(count):
                    for g in some:
                        column = left[t][g][:, 8 * p + k : 8 * p + k + 1]
                        raw[t][g - p][k] = jnp.broadcast_to(column, (8, n))
        for t in range(count):
            a, b, col, pivots = left[t][p], right[t][p], list(raw[t][0]), None
            for k in range(8):
                pivot = spread(col[k], k)
                pivots = pivot if pivots is None else jnp.where(sub == k, pivot, pivots)
                if k < 7:
                    f = jnp.where(sub > k, col[k], 0.0) * (1.0 / pivot)
                    for i in range(k + 1, 8):
                        col[i] = col[i] - f * spread(col[i], k)
                    a, b = a - f * spread(a, k), b - f * spread(b, k)
            root = lax.rsqrt(pivots)
            upper[t].append(a * root)
            lower[t].append(b * root)
            if p + 1 < end:
                ratio = 1.0 / pivots
                y, z = a * ratio, b * ratio
                for i in range(7, 0, -1):
                    f = jnp.where(sub < i, col[i] * ratio, 0.0)
                    y, z = y - f * spread(y, i), z - f * spread(z, i)
                for g in range(p + 1, end):
                    for k in range(8):
                        c = raw[t][g - p][k]
                        left[t][g] = left[t][g] - c * spread(y, k)
                        right[t][g] = right[t][g] - c * spread(z, k)
        if p + 1 == end and end < groups:
            for t in range(count):
                ah, al = halves(jnp.concatenate(upper[t][end - panel :], 0))
                bh, bl = halves(jnp.concatenate(lower[t][end - panel :], 0))
                factor = jnp.concatenate([ah, ah, al], 0)
                cut_a = dot(factor, jnp.concatenate([ah, al, ah], 0), 0, 0)
                cut_b = dot(factor, jnp.concatenate([bh, bl, bh], 0), 0, 0)
                for g in range(end, groups):
                    left[t][g] = left[t][g] - cut_a[8 * g : 8 * g + 8]
                    right[t][g] = right[t][g] - cut_b[8 * g : 8 * g + 8]
    return [jnp.concatenate(rows, 0) for rows in lower]


def join_body(right_any, left_any, out_ref, sems):
    slots = right_any.shape[0]
    copies = [
        pltpu.make_async_copy(right_any, out_ref.at[:slots], sems.at[0]),
        pltpu.make_async_copy(left_any, out_ref.at[slots:], sems.at[1]),
    ]
    for c in copies:
        c.start()
    for c in copies:
        c.wait()


def probe_body(left_any, sketch_any, out_ref, left_ref, sketch_ref, sems, *, first):
    count = out_ref.shape[0]
    copies = [pltpu.make_async_copy(sketch_any, sketch_ref, sems.at[count])]
    for k in range(count):
        copies.append(
            pltpu.make_async_copy(left_any.at[first + k], left_ref.at[k], sems.at[k])
        )
    for c in copies:
        c.start()
    copies[0].wait()
    for k in range(count):
        copies[1 + k].wait()
        for t in range(2):
            cols = slice(128 * t, 128 * t + 128)
            out_ref[k, t] = dot(left_ref[k, :, cols], sketch_ref[:, cols], 0, 0)


def early_body(place_ref, own, f1, b1, f2, b2, f3, b3, right_ref, pair_ref, pivot_ref, factor):
    group, groups = place_ref[0], place_ref[2]
    slots, n = right_ref.shape[0], own.shape[1]

    def put(ref, distance):
        at = pl.multiple_of(lax.rem(group + distance, groups) * n, n)
        for k in range(slots):
            cols = slice(128 * k, 128 * k + 128)
            if ref is None:
                factor[pl.ds(at, n), cols] = jnp.zeros((n, 128), LOW)
                pivot_ref[pl.ds(at, n), cols] = jnp.zeros((n, 128), LOW)
            else:
                factor[pl.ds(at, n), cols] = ref[k]
                pivot_ref[pl.ds(at, n), cols] = ref[k + slots]

    put(own, 0)
    for s, (f, b) in enumerate(((f1, b1), (f2, b2), (f3, b3))):
        put(f, groups - 1 - s)
        put(b, 1 + s)
    put(None, groups // 2)
    for k in range(slots):
        pair_ref[k] = dot(factor[:, 128 * k : 128 * k + 128], right_ref[k], 0, 0)


def forward_body(
    place_ref, f4, b4, early_ref, pivot_ref, probe_low, probe_high, sketch_ref, right_ref, tright_ref,
    keep_ref, send_ref, pair_ref, core_ref, part,
):
    group, live, groups, core = place_ref[0], place_ref[1], place_ref[2], place_ref[3]
    slots, n, half = right_ref.shape[0], f4.shape[1], keep_ref.shape[0]
    at = pl.multiple_of(lax.rem(group + groups // 2, groups) * n, n)
    mixed = []
    for k in range(slots):
        pair = early_ref[k] + dot(f4[k], right_ref[k, pl.ds(at, n), :], 0, 0)
        pair_ref[k] = pair
        row = []
        for t in range(2):
            cols = slice(128 * t, 128 * t + 128)
            probe = probe_low if k < probe_low.shape[0] else probe_high
            value = fine_dot(pair[:, cols], probe[k % probe_low.shape[0], t], 1, 0)
            row.append(jnp.where(k < live, -value, 0.0).astype(LOW))
        mixed.append(jnp.concatenate(row, 1))
    mixed = jnp.concatenate(mixed, 0)
    part[...] = dot(pivot_ref[...], mixed, 1, 0)
    last = jnp.concatenate([b4[k] for k in range(slots)], 1)
    part[pl.ds(at, n), :] = dot(last, mixed, 1, 0)
    cores = [
        dot(tright_ref[:, 128 * t : 128 * t + 128], sketch_ref[:, 128 * t : 128 * t + 128], 0, 0)
        for t in range(2)
    ]
    core_ref[...] = jnp.concatenate(halves(jnp.concatenate(cores, 0).reshape(half, 8, 128)), 1)
    whole = part[...].reshape(half, 2, 16, part.shape[1])
    keep_ref[...] = jnp.where(core == 0, whole[:, 0], whole[:, 1])
    send_ref[...] = jnp.where(core == 0, whole[:, 1], whole[:, 0]).astype(LOW)


def add_body(keep_ref, come_ref, out_ref):
    out_ref[...] = (keep_ref[...] + come_ref[...].astype(FULL)).astype(LOW)


def last_body(pieces_ref, direct_ref, out_ref, *, rows):
    out_ref[...] = (jnp.sum(pieces_ref[...].astype(FULL), 0) + direct_ref[...]) / rows


def merge_body(keep_ref, come_ref, core_ref, out_ref):
    width = keep_ref.shape[2]
    out_ref[:, :, :width] = (keep_ref[...] + come_ref[...].astype(FULL)).astype(LOW)
    out_ref[:, :, width:] = core_ref[...]


def own_body(pieces_ref, tleft_ref, sum_ref, out_ref):
    width = sum_ref.shape[1]
    total = jnp.sum(pieces_ref[...].astype(FULL), 0)
    sum_ref[...] = total[:, :width]
    core = jnp.concatenate(halves(total[:8, width:] + total[8:, width:]), 0)
    row = jnp.concatenate([total[:, :width].astype(LOW), tleft_ref[...], core], 1)
    out_ref[...] = jnp.broadcast_to(row[None], out_ref.shape)


def backward_body(
    place_ref, mine_ref, other_ref, own_ref, b4, pivot_ref, pair_ref, tleft_ref, tright_ref,
    left_ref, basis_ref, keep_ref, send_ref, direct_ref, turn_high, turn_low, tall,
):
    group, live, groups, core = place_ref[0], place_ref[1], place_ref[2], place_ref[3]
    slots, rows, n = left_ref.shape[0], tall.shape[0], b4.shape[1]
    width = own_ref.shape[1]

    def ordered(cols):
        mine, other = mine_ref[:, :, cols], other_ref[:, :, cols]
        even, odd = jnp.where(core == 0, mine, other), jnp.where(core == 0, other, mine)
        return jnp.concatenate([even[:, None], odd[:, None]], 1).reshape(rows, -1)

    tall[...] = ordered(slice(width, 2 * width))
    parts = mine_ref[:, :, 2 * width :].astype(FULL) + other_ref[:, :, 2 * width :].astype(FULL)
    cores = (parts[:, :8] + parts[:, 8:]).reshape(2 * 128, 128).astype(LOW)
    at = pl.multiple_of(lax.rem(group + groups // 2, groups) * n, n)
    last = jnp.concatenate([b4[k] for k in range(slots)], 1)
    whole, own, grams, seen, seen_target = [], [], [], [], []
    for t in range(2):
        cols = slice(128 * t, 128 * t + 128)
        target_core = cores[cols]
        s = ordered(cols).astype(FULL) + dot(tall[:, cols], target_core, 1, 0)
        own.append(own_ref[:, cols] + dot(tleft_ref[:, cols], target_core, 1, 0))
        turned = s.T
        high, low = halves(turned)
        grams.append(dot(high, s.astype(LOW), 1, 0) / rows)
        turn_high[t] = high
        turn_low[t] = low
    for t in range(2):
        cols = slice(128 * t, 128 * t + 128)
        both = jnp.concatenate([turn_high[t], turn_low[t]], 0)
        product = dot(both, pivot_ref[...], 1, 0)
        tail = jnp.concatenate([turn_high[t, :, pl.ds(at, n)], turn_low[t, :, pl.ds(at, n)]], 0)
        product = product + dot(tail, last, 1, 0)
        seen.append(product[:128] + product[128:])
        product = dot(both, tall[:, cols], 1, 0)
        seen_target.append(product[:128] + product[128:])
    inverse = inverse_factors(grams)
    for t in range(2):
        cols = slice(128 * t, 128 * t + 128)
        basis_ref[:, cols] = fine_dot(own[t], inverse[t], 1, 1)
        back = fine_dot(inverse[t], seen[t], 1, 0)
        total = None
        for k in range(slots):
            folded = fine_dot(back[:, 128 * k : 128 * k + 128], pair_ref[k, :, cols], 1, 0)
            folded = jnp.where(k < live, -folded, 0.0).astype(LOW)
            term = dot(left_ref[k, :, cols], folded, 1, 1)
            total = term if total is None else total + term
        total = total.reshape(keep_ref.shape[0], 2, 16, 128)
        keep_ref[:, :, cols] = jnp.where(core == 0, total[:, 0], total[:, 1])
        send_ref[:, :, cols] = jnp.where(core == 0, total[:, 1], total[:, 0]).astype(LOW)
        target_back = fine_dot(inverse[t], seen_target[t], 1, 0).astype(LOW)
        direct_ref[:, cols] = dot(tright_ref[:, cols], target_back, 1, 1)


SMEM = pl.BlockSpec(memory_space=pltpu.SMEM)
VMEM = pl.BlockSpec(memory_space=pltpu.VMEM)


def shift(x, axis, by):
    n = lax.axis_size(axis)
    return lax.ppermute(x, axis, [(i, (i + by) % n) for i in range(n)])


def near(x):
    return pltpu.with_memory_space_constraint(x, pltpu.VMEM)


def kernel(body, name, outs, scratch, place, *arrays, given=(), leave=None):
    first = () if place is None else (place,)
    return pl.pallas_call(
        body,
        in_specs=[SMEM] * len(first) + [VMEM] * (len(arrays) + len(given)),
        out_specs=[VMEM] * len(outs),
        out_shape=[
            (jax.ShapeDtypeStruct if o[0] == leave else pltpu.VMEM)(*o) for o in outs
        ],
        scratch_shapes=[pltpu.VMEM(*o) for o in scratch],
        name=name,
        compiler_params=pltpu.CompilerParams(vmem_limit_bytes=24 << 20),
    )(*first, *[near(x) for x in arrays], *given)


def probed(col_left, sketch_cols, first, count):
    return pl.pallas_call(
        functools.partial(probe_body, first=first),
        in_specs=[pl.BlockSpec(memory_space=pltpu.HBM)] * 2,
        out_specs=VMEM,
        out_shape=pltpu.VMEM((count, 2, 128, 128), FULL),
        scratch_shapes=[
            pltpu.VMEM((count, *col_left.shape[1:]), LOW),
            pltpu.VMEM(sketch_cols.shape, LOW),
            pltpu.SemaphoreType.DMA((count + 1,)),
        ],
        name="probe",
        compiler_params=pltpu.CompilerParams(vmem_limit_bytes=24 << 20),
    )(*(pltpu.with_memory_space_constraint(x, pltpu.HBM) for x in (col_left, sketch_cols)))


def shards(
    row_left, row_right, col_left, col_right, sketch_cols, target_left, target_right, live_counts
):
    slots, rows, width = col_left.shape
    block, factors = target_left.shape[0], slots * 128
    n, far, groups = lax.axis_size(INNER), INNER[:2], lax.axis_size("grp")
    half = n // 2
    place = jnp.stack(
        [lax.axis_index("grp"), live_counts[0], jnp.int32(groups), lax.axis_index(INNER[2])]
    ).astype(jnp.int32)
    own = pl.pallas_call(
        join_body,
        in_specs=[pl.BlockSpec(memory_space=pltpu.HBM)] * 2,
        out_specs=VMEM,
        out_shape=pltpu.VMEM((2 * slots, *row_left.shape[1:]), LOW),
        scratch_shapes=[pltpu.SemaphoreType.DMA((2,))],
        name="join",
        compiler_params=pltpu.CompilerParams(vmem_limit_bytes=24 << 20),
    )(*(pltpu.with_memory_space_constraint(x, pltpu.HBM) for x in (row_right, row_left)))
    chunks, probes, up, down = [own], [], own, own
    for step in range(3):
        up, down = shift(up, "grp", 1), shift(down, "grp", -1)
        if step == 0:
            own_sketch = lax.dynamic_slice_in_dim(
                sketch_cols, lax.axis_index(INNER) * block, block, 0
            )
        if step < 2:
            probe = probed(col_left, sketch_cols, step * (slots // 2), slots // 2)
            up, probe, own_sketch, place = lax.optimization_barrier(
                (up, probe, own_sketch, place)
            )
            probes.append(probe)
        chunks += [up, down]
    last_up, last_down = shift(up[:slots], "grp", 1), shift(down[slots:], "grp", -1)
    early, pivot = kernel(
        early_body,
        "early",
        [((slots, 128, width), FULL), ((rows, factors), LOW)],
        [((rows, factors), LOW)],
        place,
        *chunks,
        given=(col_right,),
    )
    piece = (half, block, width)
    keep, send, pair, core = kernel(
        forward_body,
        "forward",
        [(piece, FULL), (piece, LOW), ((slots, 128, width), FULL), ((half, block, 128), LOW)],
        [((rows, width), FULL)],
        place,
        last_up,
        last_down,
        early,
        pivot,
        *probes,
        own_sketch,
        given=(col_right, target_right),
    )
    (merged,) = kernel(
        merge_body, "merge", [((half, block, width + 128), LOW)], [], None,
        keep, shift(send, INNER[2], 1), core,
    )
    own_sum, mine = kernel(
        own_body,
        "own",
        [((block, width), FULL), ((half, block, 2 * width + 128), LOW)],
        [],
        None,
        lax.all_to_all(merged, far, 0, 0, tiled=True),
        given=(target_left,),
    )
    mine = lax.all_to_all(mine, far, 0, 0, tiled=True)
    other = shift(mine, INNER[2], 1)
    basis, keep, send, direct = kernel(
        backward_body,
        "backward",
        [((block, width), FULL), (piece, FULL), (piece, LOW), ((block, width), FULL)],
        [((2, 128, rows), LOW), ((2, 128, rows), LOW), ((rows, width), LOW)],
        place,
        mine,
        other,
        own_sum,
        last_down,
        pivot,
        pair,
        given=(target_left, target_right, col_left),
    )
    (merged,) = kernel(add_body, "add", [(piece, LOW)], [], None, keep, shift(send, INNER[2], 1))
    merged = near(merged)
    (coeffs,) = kernel(
        functools.partial(last_body, rows=rows),
        "last",
        [((block, width), FULL)],
        [],
        None,
        lax.all_to_all(merged, far, 0, 0, tiled=True),
        direct,
        leave=(block, width),
    )
    return basis, coeffs


def solution(mesh):
    finer = Mesh(
        mesh.devices.reshape(mesh.shape["grp"], 8, 4, 2), ("grp", "inner_0", "inner_1", "inner_2")
    )
    return jax.shard_map(
        shards,
        mesh=finer,
        in_specs=(
            P(INNER, "grp", None),
            P(INNER, "grp", None),
            P(INNER, None, "grp"),
            P(INNER, None, "grp"),
            P(None, "grp"),
            P(INNER, "grp"),
            P(INNER, "grp"),
            P(INNER),
        ),
        out_specs=(P(INNER, "grp"), P(INNER, "grp")),
        check_vma=False,
    )
```

```python
import functools

import jax
import jax.numpy as jnp
from jax import lax
from jax.experimental import pallas as pl
from jax.experimental.pallas import tpu as pltpu
from jax.sharding import Mesh
from jax.sharding import PartitionSpec as P

INNER = ("inner_0", "inner_1", "inner_2")
LOW = jnp.bfloat16
FULL = jnp.float32


def dot(a, b, ca, cb):
    return lax.dot_general(a, b, (((ca,), (cb,)), ((), ())), preferred_element_type=FULL)


def halves(x):
    high = x.astype(LOW)
    return high, (x - high.astype(FULL)).astype(LOW)


def fine_dot(a, b, ca, cb):
    ah, al = halves(a)
    bh, bl = halves(b)
    return dot(ah, bh, ca, cb) + (dot(ah, bl, ca, cb) + dot(al, bh, ca, cb))


def spread(x, i):
    return jnp.broadcast_to(x[i : i + 1, :], x.shape)


def inverse_factors(grams):
    n, panel = grams[0].shape[0], 4
    count, groups = len(grams), n // 8
    sub = lax.broadcasted_iota(jnp.int32, (8, n), 0)
    lane = lax.broadcasted_iota(jnp.int32, (8, n), 1)
    left = [[g[8 * i : 8 * i + 8] for i in range(groups)] for g in grams]
    right = [[(lane == sub + 8 * i).astype(FULL) for i in range(groups)] for _ in grams]
    upper, lower = [[] for _ in grams], [[] for _ in grams]
    for p in range(groups):
        end = (p // panel + 1) * panel
        raw = [[[None] * 8 for _ in range(p, end)] for _ in grams]
        for some in (range(p, p + 1), range(p + 1, end)):
            for k in range(8):
                for t in range(count):
                    for g in some:
                        column = left[t][g][:, 8 * p + k : 8 * p + k + 1]
                        raw[t][g - p][k] = jnp.broadcast_to(column, (8, n))
        for t in range(count):
            a, b, col, pivots = left[t][p], right[t][p], list(raw[t][0]), None
            for k in range(8):
                pivot = spread(col[k], k)
                pivots = pivot if pivots is None else jnp.where(sub == k, pivot, pivots)
                if k < 7:
                    f = jnp.where(sub > k, col[k], 0.0) * (1.0 / pivot)
                    for i in range(k + 1, 8):
                        col[i] = col[i] - f * spread(col[i], k)
                    a, b = a - f * spread(a, k), b - f * spread(b, k)
            root = lax.rsqrt(pivots)
            upper[t].append(a * root)
            lower[t].append(b * root)
            if p + 1 < end:
                ratio = 1.0 / pivots
                y, z = a * ratio, b * ratio
                for i in range(7, 0, -1):
                    f = jnp.where(sub < i, col[i] * ratio, 0.0)
                    y, z = y - f * spread(y, i), z - f * spread(z, i)
                for g in range(p + 1, end):
                    for k in range(8):
                        c = raw[t][g - p][k]
                        left[t][g] = left[t][g] - c * spread(y, k)
                        right[t][g] = right[t][g] - c * spread(z, k)
        if p + 1 == end and end < groups:
            for t in range(count):
                ah, al = halves(jnp.concatenate(upper[t][end - panel :], 0))
                bh, bl = halves(jnp.concatenate(lower[t][end - panel :], 0))
                factor = jnp.concatenate([ah, ah, al], 0)
                cut_a = dot(factor, jnp.concatenate([ah, al, ah], 0), 0, 0)
                cut_b = dot(factor, jnp.concatenate([bh, bl, bh], 0), 0, 0)
                for g in range(end, groups):
                    left[t][g] = left[t][g] - cut_a[8 * g : 8 * g + 8]
                    right[t][g] = right[t][g] - cut_b[8 * g : 8 * g + 8]
    return [jnp.concatenate(rows, 0) for rows in lower]


def join_body(right_any, left_any, out_ref, sems):
    slots = right_any.shape[0]
    copies = [
        pltpu.make_async_copy(right_any, out_ref.at[:slots], sems.at[0]),
        pltpu.make_async_copy(left_any, out_ref.at[slots:], sems.at[1]),
    ]
    for c in copies:
        c.start()
    for c in copies:
        c.wait()


def probe_body(left_any, sketch_any, out_ref, left_ref, sketch_ref, sems, *, first):
    count = out_ref.shape[0]
    copies = [pltpu.make_async_copy(sketch_any, sketch_ref, sems.at[count])]
    for k in range(count):
        copies.append(
            pltpu.make_async_copy(left_any.at[first + k], left_ref.at[k], sems.at[k])
        )
    for c in copies:
        c.start()
    copies[0].wait()
    for k in range(count):
        copies[1 + k].wait()
        for t in range(2):
            cols = slice(128 * t, 128 * t + 128)
            out_ref[k, t] = dot(left_ref[k, :, cols], sketch_ref[:, cols], 0, 0)


def early_body(place_ref, own, f1, b1, f2, b2, f3, b3, right_ref, pair_ref, pivot_ref, factor):
    group, groups = place_ref[0], place_ref[2]
    slots, n = right_ref.shape[0], own.shape[1]

    def put(ref, distance):
        at = pl.multiple_of(lax.rem(group + distance, groups) * n, n)
        for k in range(slots):
            cols = slice(128 * k, 128 * k + 128)
            if ref is None:
                factor[pl.ds(at, n), cols] = jnp.zeros((n, 128), LOW)
                pivot_ref[pl.ds(at, n), cols] = jnp.zeros((n, 128), LOW)
            else:
                factor[pl.ds(at, n), cols] = ref[k]
                pivot_ref[pl.ds(at, n), cols] = ref[k + slots]

    put(own, 0)
    odd = lax.rem(group, 2) == 1
    for s, (f, b) in enumerate(((f1, b1), (f2, b2), (f3, b3))):
        put(f, jnp.where(odd, groups - 1 - s, 1 + s))
        put(b, jnp.where(odd, 1 + s, groups - 1 - s))
    put(None, groups // 2)
    for k in range(slots):
        pair_ref[k] = dot(factor[:, 128 * k : 128 * k + 128], right_ref[k], 0, 0)


def forward_body(
    place_ref, f4, b4, early_ref, pivot_ref, probe_low, probe_high, sketch_ref, right_ref, tright_ref,
    keep_ref, send_ref, pair_ref, core_ref, part,
):
    group, live, groups, core = place_ref[0], place_ref[1], place_ref[2], place_ref[3]
    slots, n, half = right_ref.shape[0], f4.shape[1], keep_ref.shape[0]
    at = pl.multiple_of(lax.rem(group + groups // 2, groups) * n, n)
    mixed = []
    for k in range(slots):
        pair = early_ref[k] + dot(f4[k], right_ref[k, pl.ds(at, n), :], 0, 0)
        pair_ref[k] = pair
        row = []
        for t in range(2):
            cols = slice(128 * t, 128 * t + 128)
            probe = probe_low if k < probe_low.shape[0] else probe_high
            value = fine_dot(pair[:, cols], probe[k % probe_low.shape[0], t], 1, 0)
            row.append(jnp.where(k < live, -value, 0.0).astype(LOW))
        mixed.append(jnp.concatenate(row, 1))
    mixed = jnp.concatenate(mixed, 0)
    part[...] = dot(pivot_ref[...], mixed, 1, 0)
    last = jnp.concatenate([b4[k] for k in range(slots)], 1)
    part[pl.ds(at, n), :] = dot(last, mixed, 1, 0)
    cores = [
        dot(tright_ref[:, 128 * t : 128 * t + 128], sketch_ref[:, 128 * t : 128 * t + 128], 0, 0)
        for t in range(2)
    ]
    core_ref[...] = jnp.concatenate(halves(jnp.concatenate(cores, 0).reshape(half, 8, 128)), 1)
    whole = part[...].reshape(half, 2, 16, part.shape[1])
    keep_ref[...] = jnp.where(core == 0, whole[:, 0], whole[:, 1])
    send_ref[...] = jnp.where(core == 0, whole[:, 1], whole[:, 0]).astype(LOW)


def add_body(keep_ref, come_ref, out_ref):
    out_ref[...] = (keep_ref[...] + come_ref[...].astype(FULL)).astype(LOW)


def last_body(pieces_ref, direct_ref, out_ref, *, rows):
    out_ref[...] = (jnp.sum(pieces_ref[...].astype(FULL), 0) + direct_ref[...]) / rows


def merge_body(keep_ref, come_ref, core_ref, out_ref):
    width = keep_ref.shape[2]
    out_ref[:, :, :width] = (keep_ref[...] + come_ref[...].astype(FULL)).astype(LOW)
    out_ref[:, :, width:] = core_ref[...]


def own_body(pieces_ref, tleft_ref, sum_ref, out_ref):
    width = sum_ref.shape[1]
    total = jnp.sum(pieces_ref[...].astype(FULL), 0)
    sum_ref[...] = total[:, :width]
    core = jnp.concatenate(halves(total[:8, width:] + total[8:, width:]), 0)
    row = jnp.concatenate([total[:, :width].astype(LOW), tleft_ref[...], core], 1)
    out_ref[...] = jnp.broadcast_to(row[None], out_ref.shape)


def backward_body(
    place_ref, mine_ref, other_ref, own_ref, b4, pivot_ref, pair_ref, tleft_ref, tright_ref,
    left_ref, basis_ref, keep_ref, send_ref, direct_ref, turn_high, turn_low, tall,
):
    group, live, groups, core = place_ref[0], place_ref[1], place_ref[2], place_ref[3]
    slots, rows, n = left_ref.shape[0], tall.shape[0], b4.shape[1]
    width = own_ref.shape[1]

    def ordered(cols):
        mine, other = mine_ref[:, :, cols], other_ref[:, :, cols]
        even, odd = jnp.where(core == 0, mine, other), jnp.where(core == 0, other, mine)
        return jnp.concatenate([even[:, None], odd[:, None]], 1).reshape(rows, -1)

    tall[...] = ordered(slice(width, 2 * width))
    parts = mine_ref[:, :, 2 * width :].astype(FULL) + other_ref[:, :, 2 * width :].astype(FULL)
    cores = (parts[:, :8] + parts[:, 8:]).reshape(2 * 128, 128).astype(LOW)
    at = pl.multiple_of(lax.rem(group + groups // 2, groups) * n, n)
    last = jnp.concatenate([b4[k] for k in range(slots)], 1)
    whole, own, grams, seen, seen_target = [], [], [], [], []
    for t in range(2):
        cols = slice(128 * t, 128 * t + 128)
        target_core = cores[cols]
        s = ordered(cols).astype(FULL) + dot(tall[:, cols], target_core, 1, 0)
        own.append(own_ref[:, cols] + dot(tleft_ref[:, cols], target_core, 1, 0))
        turned = s.T
        high, low = halves(turned)
        grams.append(dot(high, s.astype(LOW), 1, 0) / rows)
        turn_high[t] = high
        turn_low[t] = low
    for t in range(2):
        cols = slice(128 * t, 128 * t + 128)
        both = jnp.concatenate([turn_high[t], turn_low[t]], 0)
        product = dot(both, pivot_ref[...], 1, 0)
        tail = jnp.concatenate([turn_high[t, :, pl.ds(at, n)], turn_low[t, :, pl.ds(at, n)]], 0)
        product = product + dot(tail, last, 1, 0)
        seen.append(product[:128] + product[128:])
        product = dot(both, tall[:, cols], 1, 0)
        seen_target.append(product[:128] + product[128:])
    inverse = inverse_factors(grams)
    for t in range(2):
        cols = slice(128 * t, 128 * t + 128)
        basis_ref[:, cols] = fine_dot(own[t], inverse[t], 1, 1)
        back = fine_dot(inverse[t], seen[t], 1, 0)
        total = None
        for k in range(slots):
            folded = fine_dot(back[:, 128 * k : 128 * k + 128], pair_ref[k, :, cols], 1, 0)
            folded = jnp.where(k < live, -folded, 0.0).astype(LOW)
            term = dot(left_ref[k, :, cols], folded, 1, 1)
            total = term if total is None else total + term
        total = total.reshape(keep_ref.shape[0], 2, 16, 128)
        keep_ref[:, :, cols] = jnp.where(core == 0, total[:, 0], total[:, 1])
        send_ref[:, :, cols] = jnp.where(core == 0, total[:, 1], total[:, 0]).astype(LOW)
        target_back = fine_dot(inverse[t], seen_target[t], 1, 0).astype(LOW)
        direct_ref[:, cols] = dot(tright_ref[:, cols], target_back, 1, 1)


SMEM = pl.BlockSpec(memory_space=pltpu.SMEM)
VMEM = pl.BlockSpec(memory_space=pltpu.VMEM)


def shift(x, axis, by):
    n = lax.axis_size(axis)
    return lax.ppermute(x, axis, [(i, (i + by) % n) for i in range(n)])


def paired(x, axis, first):
    n = lax.axis_size(axis)
    return lax.ppermute(x, axis, [(i, (i + 1 - 2 * ((i + first) % 2)) % n) for i in range(n)])


def near(x):
    return pltpu.with_memory_space_constraint(x, pltpu.VMEM)


def kernel(body, name, outs, scratch, place, *arrays, given=(), leave=None):
    first = () if place is None else (place,)
    return pl.pallas_call(
        body,
        in_specs=[SMEM] * len(first) + [VMEM] * (len(arrays) + len(given)),
        out_specs=[VMEM] * len(outs),
        out_shape=[
            (jax.ShapeDtypeStruct if o[0] == leave else pltpu.VMEM)(*o) for o in outs
        ],
        scratch_shapes=[pltpu.VMEM(*o) for o in scratch],
        name=name,
        compiler_params=pltpu.CompilerParams(vmem_limit_bytes=24 << 20),
    )(*first, *[near(x) for x in arrays], *given)


def probed(col_left, sketch_cols, first, count):
    return pl.pallas_call(
        functools.partial(probe_body, first=first),
        in_specs=[pl.BlockSpec(memory_space=pltpu.HBM)] * 2,
        out_specs=VMEM,
        out_shape=pltpu.VMEM((count, 2, 128, 128), FULL),
        scratch_shapes=[
            pltpu.VMEM((count, *col_left.shape[1:]), LOW),
            pltpu.VMEM(sketch_cols.shape, LOW),
            pltpu.SemaphoreType.DMA((count + 1,)),
        ],
        name="probe",
        compiler_params=pltpu.CompilerParams(vmem_limit_bytes=24 << 20),
    )(*(pltpu.with_memory_space_constraint(x, pltpu.HBM) for x in (col_left, sketch_cols)))


def shards(
    row_left, row_right, col_left, col_right, sketch_cols, target_left, target_right, live_counts
):
    slots, rows, width = col_left.shape
    block, factors = target_left.shape[0], slots * 128
    n, far, groups = lax.axis_size(INNER), INNER[:2], lax.axis_size("grp")
    half = n // 2
    place = jnp.stack(
        [lax.axis_index("grp"), live_counts[0], jnp.int32(groups), lax.axis_index(INNER[2])]
    ).astype(jnp.int32)
    own = pl.pallas_call(
        join_body,
        in_specs=[pl.BlockSpec(memory_space=pltpu.HBM)] * 2,
        out_specs=VMEM,
        out_shape=pltpu.VMEM((2 * slots, *row_left.shape[1:]), LOW),
        scratch_shapes=[pltpu.SemaphoreType.DMA((2,))],
        name="join",
        compiler_params=pltpu.CompilerParams(vmem_limit_bytes=24 << 20),
    )(*(pltpu.with_memory_space_constraint(x, pltpu.HBM) for x in (row_right, row_left)))
    chunks, probes, here, there = [own], [], own, own
    for step in range(3):
        here, there = paired(here, "grp", 0), paired(there, "grp", 1)
        if step == 0:
            own_sketch = lax.dynamic_slice_in_dim(
                sketch_cols, lax.axis_index(INNER) * block, block, 0
            )
        if step < 2:
            probe = probed(col_left, sketch_cols, step * (slots // 2), slots // 2)
            here, probe, own_sketch, place = lax.optimization_barrier(
                (here, probe, own_sketch, place)
            )
            probes.append(probe)
        chunks += [here, there]
        here, there = there, here
    last_right, last_left = paired(here[:slots], "grp", 0), paired(there[slots:], "grp", 1)
    early, pivot = kernel(
        early_body,
        "early",
        [((slots, 128, width), FULL), ((rows, factors), LOW)],
        [((rows, factors), LOW)],
        place,
        *chunks,
        given=(col_right,),
    )
    piece = (half, block, width)
    keep, send, pair, core = kernel(
        forward_body,
        "forward",
        [(piece, FULL), (piece, LOW), ((slots, 128, width), FULL), ((half, block, 128), LOW)],
        [((rows, width), FULL)],
        place,
        last_right,
        last_left,
        early,
        pivot,
        *probes,
        own_sketch,
        given=(col_right, target_right),
    )
    (merged,) = kernel(
        merge_body, "merge", [((half, block, width + 128), LOW)], [], None,
        keep, shift(send, INNER[2], 1), core,
    )
    own_sum, mine = kernel(
        own_body,
        "own",
        [((block, width), FULL), ((half, block, 2 * width + 128), LOW)],
        [],
        None,
        lax.all_to_all(merged, far, 0, 0, tiled=True),
        given=(target_left,),
    )
    mine = lax.all_to_all(mine, far, 0, 0, tiled=True)
    other = shift(mine, INNER[2], 1)
    basis, keep, send, direct = kernel(
        backward_body,
        "backward",
        [((block, width), FULL), (piece, FULL), (piece, LOW), ((block, width), FULL)],
        [((2, 128, rows), LOW), ((2, 128, rows), LOW), ((rows, width), LOW)],
        place,
        mine,
        other,
        own_sum,
        last_left,
        pivot,
        pair,
        given=(target_left, target_right, col_left),
    )
    (merged,) = kernel(add_body, "add", [(piece, LOW)], [], None, keep, shift(send, INNER[2], 1))
    merged = near(merged)
    (coeffs,) = kernel(
        functools.partial(last_body, rows=rows),
        "last",
        [((block, width), FULL)],
        [],
        None,
        lax.all_to_all(merged, far, 0, 0, tiled=True),
        direct,
        leave=(block, width),
    )
    return basis, coeffs


def solution(mesh):
    finer = Mesh(
        mesh.devices.reshape(mesh.shape["grp"], 8, 4, 2), ("grp", "inner_0", "inner_1", "inner_2")
    )
    return jax.shard_map(
        shards,
        mesh=finer,
        in_specs=(
            P(INNER, "grp", None),
            P(INNER, "grp", None),
            P(INNER, None, "grp"),
            P(INNER, None, "grp"),
            P(None, "grp"),
            P(INNER, "grp"),
            P(INNER, "grp"),
            P(INNER),
        ),
        out_specs=(P(INNER, "grp"), P(INNER, "grp")),
        check_vma=False,
    )
```

```python
import functools

import jax
import jax.numpy as jnp
from jax import lax
from jax.experimental import pallas as pl
from jax.experimental.pallas import tpu as pltpu
from jax.sharding import Mesh
from jax.sharding import PartitionSpec as P

INNER = ("inner_0", "inner_1", "inner_2")
LOW = jnp.bfloat16
FULL = jnp.float32


def dot(a, b, ca, cb):
    return lax.dot_general(a, b, (((ca,), (cb,)), ((), ())), preferred_element_type=FULL)


def halves(x):
    high = x.astype(LOW)
    return high, (x - high.astype(FULL)).astype(LOW)


def fine_dot(a, b, ca, cb):
    ah, al = halves(a)
    bh, bl = halves(b)
    return dot(ah, bh, ca, cb) + (dot(ah, bl, ca, cb) + dot(al, bh, ca, cb))


def spread(x, i):
    return jnp.broadcast_to(x[i : i + 1, :], x.shape)


def inverse_factors(grams):
    n, panel = grams[0].shape[0], 4
    count, groups = len(grams), n // 8
    sub = lax.broadcasted_iota(jnp.int32, (8, n), 0)
    lane = lax.broadcasted_iota(jnp.int32, (8, n), 1)
    left = [[g[8 * i : 8 * i + 8] for i in range(groups)] for g in grams]
    right = [[(lane == sub + 8 * i).astype(FULL) for i in range(groups)] for _ in grams]
    upper, lower = [[] for _ in grams], [[] for _ in grams]
    for p in range(groups):
        end = (p // panel + 1) * panel
        raw = [[[None] * 8 for _ in range(p, end)] for _ in grams]
        for some in (range(p, p + 1), range(p + 1, end)):
            for k in range(8):
                for t in range(count):
                    for g in some:
                        column = left[t][g][:, 8 * p + k : 8 * p + k + 1]
                        raw[t][g - p][k] = jnp.broadcast_to(column, (8, n))
        for t in range(count):
            a, b, col, pivots = left[t][p], right[t][p], list(raw[t][0]), None
            for k in range(8):
                pivot = spread(col[k], k)
                pivots = pivot if pivots is None else jnp.where(sub == k, pivot, pivots)
                if k < 7:
                    f = jnp.where(sub > k, col[k], 0.0) * (1.0 / pivot)
                    for i in range(k + 1, 8):
                        col[i] = col[i] - f * spread(col[i], k)
                    a, b = a - f * spread(a, k), b - f * spread(b, k)
            root = lax.rsqrt(pivots)
            upper[t].append(a * root)
            lower[t].append(b * root)
            if p + 1 < end:
                ratio = 1.0 / pivots
                y, z = a * ratio, b * ratio
                for i in range(7, 0, -1):
                    f = jnp.where(sub < i, col[i] * ratio, 0.0)
                    y, z = y - f * spread(y, i), z - f * spread(z, i)
                for g in range(p + 1, end):
                    for k in range(8):
                        c = raw[t][g - p][k]
                        left[t][g] = left[t][g] - c * spread(y, k)
                        right[t][g] = right[t][g] - c * spread(z, k)
        if p + 1 == end and end < groups:
            for t in range(count):
                ah, al = halves(jnp.concatenate(upper[t][end - panel :], 0))
                bh, bl = halves(jnp.concatenate(lower[t][end - panel :], 0))
                factor = jnp.concatenate([ah, ah, al], 0)
                cut_a = dot(factor, jnp.concatenate([ah, al, ah], 0), 0, 0)
                cut_b = dot(factor, jnp.concatenate([bh, bl, bh], 0), 0, 0)
                for g in range(end, groups):
                    left[t][g] = left[t][g] - cut_a[8 * g : 8 * g + 8]
                    right[t][g] = right[t][g] - cut_b[8 * g : 8 * g + 8]
    return [jnp.concatenate(rows, 0) for rows in lower]


def join_body(right_any, left_any, out_ref, sems):
    slots = right_any.shape[0]
    copies = [
        pltpu.make_async_copy(right_any, out_ref.at[:slots], sems.at[0]),
        pltpu.make_async_copy(left_any, out_ref.at[slots:], sems.at[1]),
    ]
    for c in copies:
        c.start()
    for c in copies:
        c.wait()


def probe_body(
    place_ref, left_any, sketch_any, out_ref, own_ref, left_ref, sketch_ref, sems, *, first
):
    count = out_ref.shape[0]
    copies = [pltpu.make_async_copy(sketch_any, sketch_ref, sems.at[count])]
    for k in range(count):
        copies.append(
            pltpu.make_async_copy(left_any.at[first + k], left_ref.at[k], sems.at[k])
        )
    for c in copies:
        c.start()
    copies[0].wait()
    lines = own_ref.shape[0]
    own_ref[...] = sketch_ref[pl.ds(pl.multiple_of(place_ref[4] * lines, lines), lines), :]
    for k in range(count):
        copies[1 + k].wait()
        for t in range(2):
            cols = slice(128 * t, 128 * t + 128)
            out_ref[k, t] = dot(left_ref[k, :, cols], sketch_ref[:, cols], 0, 0)


def early_body(place_ref, own, f1, b1, f2, b2, f3, b3, right_ref, pair_ref, pivot_ref, factor):
    group, groups = place_ref[0], place_ref[2]
    slots, n = right_ref.shape[0], own.shape[1]

    def put(ref, distance):
        at = pl.multiple_of(lax.rem(group + distance, groups) * n, n)
        for k in range(slots):
            cols = slice(128 * k, 128 * k + 128)
            if ref is None:
                factor[pl.ds(at, n), cols] = jnp.zeros((n, 128), LOW)
                pivot_ref[pl.ds(at, n), cols] = jnp.zeros((n, 128), LOW)
            else:
                factor[pl.ds(at, n), cols] = ref[k]
                pivot_ref[pl.ds(at, n), cols] = ref[k + slots]

    put(own, 0)
    for s, (f, b) in enumerate(((f1, b1), (f2, b2), (f3, b3))):
        put(f, groups - 1 - s)
        put(b, 1 + s)
    put(None, groups // 2)
    for k in range(slots):
        pair_ref[k] = dot(factor[:, 128 * k : 128 * k + 128], right_ref[k], 0, 0)


def upper_lines(shape):
    return lax.broadcasted_iota(jnp.int32, shape, 1) < 4


def packed(x):
    x = x.reshape(16, 8, 128)
    high = x.astype(LOW).astype(FULL)
    low, top = x - high, upper_lines(x.shape)
    even = jnp.where(top, high, pltpu.roll(low, 4, 1))
    odd = jnp.where(top, pltpu.roll(high, 4, 1), low)
    return jnp.concatenate([even[:, None], odd[:, None]], 1).reshape(32, 8, 128)


def repacked(x):
    total = x + pltpu.roll(x, 4, 1)
    high = total.astype(LOW).astype(FULL)
    return jnp.where(upper_lines(x.shape), high, total - high)


def unpacked(x):
    total = (x + pltpu.roll(x, 4, 1)).reshape(16, 2, 8, 128)
    even, odd = total[:, 0], total[:, 1]
    return jnp.where(upper_lines(even.shape), even, odd).reshape(128, 128)


def forward_body(
    place_ref, f4, b4, early_ref, pivot_ref, probe_low, probe_high, sketch_ref, right_ref, tright_ref,
    keep_ref, send_ref, pair_ref, part,
):
    group, live, groups, core = place_ref[0], place_ref[1], place_ref[2], place_ref[3]
    slots, n, half = right_ref.shape[0], f4.shape[1], keep_ref.shape[0]
    at = pl.multiple_of(lax.rem(group + groups // 2, groups) * n, n)
    mixed = []
    for k in range(slots):
        pair = early_ref[k] + dot(f4[k], right_ref[k, pl.ds(at, n), :], 0, 0)
        pair_ref[k] = pair
        row = []
        for t in range(2):
            cols = slice(128 * t, 128 * t + 128)
            probe = probe_low if k < probe_low.shape[0] else probe_high
            value = fine_dot(pair[:, cols], probe[k % probe_low.shape[0], t], 1, 0)
            row.append(jnp.where(k < live, -value, 0.0).astype(LOW))
        mixed.append(jnp.concatenate(row, 1))
    mixed = jnp.concatenate(mixed, 0)
    part[...] = dot(pivot_ref[...], mixed, 1, 0)
    last = jnp.concatenate([b4[k] for k in range(slots)], 1)
    part[pl.ds(at, n), :] = dot(last, mixed, 1, 0)
    cores = [
        dot(tright_ref[:, 128 * t : 128 * t + 128], sketch_ref[:, 128 * t : 128 * t + 128], 0, 0)
        for t in range(2)
    ]
    for t in range(2):
        whole = part[:, 128 * t : 128 * t + 128].reshape(half, 2, 16, 128)
        lines = slice(16 * t, 16 * t + 16)
        keep_ref[:, lines] = jnp.where(core == 0, whole[:, 0], whole[:, 1])
        send_ref[:, lines] = jnp.where(core == 0, whole[:, 1], whole[:, 0]).astype(LOW)
    keep_ref[:, 32:] = packed(jnp.where(core == 0, cores[0], cores[1]))
    send_ref[:, 32:] = packed(jnp.where(core == 0, cores[1], cores[0])).astype(LOW)


def add_body(keep_ref, come_ref, out_ref):
    out_ref[...] = (keep_ref[...] + come_ref[...].astype(FULL)).astype(LOW)


def last_body(pieces_ref, direct_ref, out_ref, *, rows):
    out_ref[...] = (jnp.sum(pieces_ref[...].astype(FULL), 0) + direct_ref[...]) / rows


def merge_body(keep_ref, come_ref, out_ref):
    total = keep_ref[...] + come_ref[...].astype(FULL)
    out_ref[:, :32] = total[:, :32].astype(LOW)
    out_ref[:, 32:] = repacked(total[:, 32:]).astype(LOW)


def own_body(pieces_ref, tleft_ref, sum_ref, out_ref):
    total = jnp.sum(pieces_ref[...].astype(FULL), 0)
    sum_ref[...] = jnp.concatenate([total[:16], total[16:32]], 1)
    lines = jnp.concatenate(
        [
            total[:32].astype(LOW),
            tleft_ref[:, :128],
            tleft_ref[:, 128:],
            repacked(total[None, 32:])[0].astype(LOW),
        ],
        0,
    )
    out_ref[...] = jnp.broadcast_to(lines[None], out_ref.shape)


def backward_body(
    place_ref, mine_ref, other_ref, own_ref, b4, pivot_ref, pair_ref, tleft_ref, tright_ref,
    left_ref, basis_ref, keep_ref, send_ref, direct_ref, turn_high, turn_low, tall,
):
    group, live, groups, core = place_ref[0], place_ref[1], place_ref[2], place_ref[3]
    slots, rows, n = left_ref.shape[0], tall.shape[0], b4.shape[1]

    def ordered(first):
        mine, other = mine_ref[:, first : first + 16], other_ref[:, first : first + 16]
        even, odd = jnp.where(core == 0, mine, other), jnp.where(core == 0, other, mine)
        return jnp.concatenate([even[:, None], odd[:, None]], 1).reshape(rows, -1)

    blocks = [mine_ref[:, 64:].astype(FULL), other_ref[:, 64:].astype(FULL)]
    at = pl.multiple_of(lax.rem(group + groups // 2, groups) * n, n)
    last = jnp.concatenate([b4[k] for k in range(slots)], 1)
    whole, own, grams, seen, seen_target = [], [], [], [], []
    for t in range(2):
        cols = slice(128 * t, 128 * t + 128)
        block = jnp.where(core == t, blocks[0], blocks[1])
        target_core = unpacked(block).astype(LOW)
        tall[:, cols] = ordered(32 + 16 * t)
        s = ordered(16 * t).astype(FULL) + dot(tall[:, cols], target_core, 1, 0)
        own.append(own_ref[:, cols] + dot(tleft_ref[:, cols], target_core, 1, 0))
        turned = s.T
        high, low = halves(turned)
        grams.append(dot(high, s.astype(LOW), 1, 0) / rows)
        turn_high[t] = high
        turn_low[t] = low
    for t in range(2):
        cols = slice(128 * t, 128 * t + 128)
        both = jnp.concatenate([turn_high[t], turn_low[t]], 0)
        product = dot(both, pivot_ref[...], 1, 0)
        tail = jnp.concatenate([turn_high[t, :, pl.ds(at, n)], turn_low[t, :, pl.ds(at, n)]], 0)
        product = product + dot(tail, last, 1, 0)
        seen.append(product[:128] + product[128:])
        product = dot(both, tall[:, cols], 1, 0)
        seen_target.append(product[:128] + product[128:])
    inverse = inverse_factors(grams)
    for t in range(2):
        cols = slice(128 * t, 128 * t + 128)
        basis_ref[:, cols] = fine_dot(own[t], inverse[t], 1, 1)
        back = fine_dot(inverse[t], seen[t], 1, 0)
        total = None
        for k in range(slots):
            folded = fine_dot(back[:, 128 * k : 128 * k + 128], pair_ref[k, :, cols], 1, 0)
            folded = jnp.where(k < live, -folded, 0.0).astype(LOW)
            term = dot(left_ref[k, :, cols], folded, 1, 1)
            total = term if total is None else total + term
        total = total.reshape(keep_ref.shape[0], 2, 16, 128)
        keep_ref[:, :, cols] = jnp.where(core == 0, total[:, 0], total[:, 1])
        send_ref[:, :, cols] = jnp.where(core == 0, total[:, 1], total[:, 0]).astype(LOW)
        target_back = fine_dot(inverse[t], seen_target[t], 1, 0).astype(LOW)
        direct_ref[:, cols] = dot(tright_ref[:, cols], target_back, 1, 1)


SMEM = pl.BlockSpec(memory_space=pltpu.SMEM)
VMEM = pl.BlockSpec(memory_space=pltpu.VMEM)


def shift(x, axis, by):
    n = lax.axis_size(axis)
    return lax.ppermute(x, axis, [(i, (i + by) % n) for i in range(n)])


def near(x):
    return pltpu.with_memory_space_constraint(x, pltpu.VMEM)


def kernel(body, name, outs, scratch, place, *arrays, given=(), leave=None):
    first = () if place is None else (place,)
    return pl.pallas_call(
        body,
        in_specs=[SMEM] * len(first) + [VMEM] * (len(arrays) + len(given)),
        out_specs=[VMEM] * len(outs),
        out_shape=[
            (jax.ShapeDtypeStruct if o[0] == leave else pltpu.VMEM)(*o) for o in outs
        ],
        scratch_shapes=[pltpu.VMEM(*o) for o in scratch],
        name=name,
        compiler_params=pltpu.CompilerParams(vmem_limit_bytes=16 << 20),
    )(*first, *[near(x) for x in arrays], *given)


def probed(place, col_left, sketch_cols, block, first, count):
    return pl.pallas_call(
        functools.partial(probe_body, first=first),
        in_specs=[SMEM] + [pl.BlockSpec(memory_space=pltpu.HBM)] * 2,
        out_specs=[VMEM] * 2,
        out_shape=[
            pltpu.VMEM((count, 2, 128, 128), FULL),
            pltpu.VMEM((block, sketch_cols.shape[1]), LOW),
        ],
        scratch_shapes=[
            pltpu.VMEM((count, *col_left.shape[1:]), LOW),
            pltpu.VMEM(sketch_cols.shape, LOW),
            pltpu.SemaphoreType.DMA((count + 1,)),
        ],
        name="probe",
        compiler_params=pltpu.CompilerParams(vmem_limit_bytes=16 << 20),
    )(place, *(pltpu.with_memory_space_constraint(x, pltpu.HBM) for x in (col_left, sketch_cols)))


def shards(
    row_left, row_right, col_left, col_right, sketch_cols, target_left, target_right, live_counts
):
    slots, rows, width = col_left.shape
    block, factors = target_left.shape[0], slots * 128
    n, far, groups = lax.axis_size(INNER), INNER[:2], lax.axis_size("grp")
    half = n // 2
    place = jnp.stack(
        [
            lax.axis_index("grp"),
            live_counts[0],
            jnp.int32(groups),
            lax.axis_index(INNER[2]),
            lax.axis_index(INNER),
        ]
    ).astype(jnp.int32)
    own = pl.pallas_call(
        join_body,
        in_specs=[pl.BlockSpec(memory_space=pltpu.HBM)] * 2,
        out_specs=VMEM,
        out_shape=pltpu.VMEM((2 * slots, *row_left.shape[1:]), LOW),
        scratch_shapes=[pltpu.SemaphoreType.DMA((2,))],
        name="join",
        compiler_params=pltpu.CompilerParams(vmem_limit_bytes=16 << 20),
    )(*(pltpu.with_memory_space_constraint(x, pltpu.HBM) for x in (row_right, row_left)))
    chunks, probes, up, down = [own], [], own, own
    for step in range(3):
        up, down = shift(up, "grp", 1), shift(down, "grp", -1)
        if step != 1:
            half_slots = slots // 2
            probe, own_sketch = probed(
                place, col_left, sketch_cols, block, step // 2 * half_slots, half_slots
            )
            up, probe = lax.optimization_barrier((up, probe))
            probes.append(probe)
        chunks += [up, down]
    last_up, last_down = shift(up[:slots], "grp", 1), shift(down[slots:], "grp", -1)
    early, pivot = kernel(
        early_body,
        "early",
        [((slots, 128, width), FULL), ((rows, factors), LOW)],
        [((rows, factors), LOW)],
        place,
        *chunks,
        given=(col_right,),
    )
    piece = (half, block, width)
    keep, send, pair = kernel(
        forward_body,
        "forward",
        [((half, 40, 128), FULL), ((half, 40, 128), LOW), ((slots, 128, width), FULL)],
        [((rows, width), FULL)],
        place,
        last_up,
        last_down,
        early,
        pivot,
        *probes,
        own_sketch,
        given=(col_right, target_right),
    )
    (merged,) = kernel(
        merge_body, "merge", [((half, 40, 128), LOW)], [], None, keep, shift(send, INNER[2], 1)
    )
    own_sum, mine = kernel(
        own_body,
        "own",
        [((block, width), FULL), ((half, 72, 128), LOW)],
        [],
        None,
        lax.all_to_all(merged, far, 0, 0, tiled=True),
        given=(target_left,),
    )
    mine = lax.all_to_all(mine, far, 0, 0, tiled=True)
    other = shift(mine, INNER[2], 1)
    basis, keep, send, direct = kernel(
        backward_body,
        "backward",
        [((block, width), FULL), (piece, FULL), (piece, LOW), ((block, width), FULL)],
        [((2, 128, rows), LOW), ((2, 128, rows), LOW), ((rows, width), LOW)],
        place,
        mine,
        other,
        own_sum,
        last_down,
        pivot,
        pair,
        given=(target_left, target_right, col_left),
    )
    (merged,) = kernel(add_body, "add", [(piece, LOW)], [], None, keep, shift(send, INNER[2], 1))
    merged = near(merged)
    (coeffs,) = kernel(
        functools.partial(last_body, rows=rows),
        "last",
        [((block, width), FULL)],
        [],
        None,
        lax.all_to_all(merged, far, 0, 0, tiled=True),
        direct,
        leave=(block, width),
    )
    return basis, coeffs


def solution(mesh):
    finer = Mesh(
        mesh.devices.reshape(mesh.shape["grp"], 8, 4, 2), ("grp", "inner_0", "inner_1", "inner_2")
    )
    return jax.shard_map(
        shards,
        mesh=finer,
        in_specs=(
            P(INNER, "grp", None),
            P(INNER, "grp", None),
            P(INNER, None, "grp"),
            P(INNER, None, "grp"),
            P(None, "grp"),
            P(INNER, "grp"),
            P(INNER, "grp"),
            P(INNER),
        ),
        out_specs=(P(INNER, "grp"), P(INNER, "grp")),
        check_vma=False,
    )
```

```python
import functools

import jax
import jax.numpy as jnp
from jax import lax
from jax.experimental import pallas as pl
from jax.experimental.pallas import tpu as pltpu
from jax.sharding import Mesh
from jax.sharding import PartitionSpec as P

INNER = ("inner_0", "inner_1", "inner_2")
LOW = jnp.bfloat16
FULL = jnp.float32


def dot(a, b, ca, cb):
    return lax.dot_general(a, b, (((ca,), (cb,)), ((), ())), preferred_element_type=FULL)


def halves(x):
    high = x.astype(LOW)
    return high, (x - high.astype(FULL)).astype(LOW)


def fine_dot(a, b, ca, cb):
    ah, al = halves(a)
    bh, bl = halves(b)
    return dot(ah, bh, ca, cb) + (dot(ah, bl, ca, cb) + dot(al, bh, ca, cb))


def spread(x, i):
    return jnp.broadcast_to(x[i : i + 1, :], x.shape)


def inverse_factors(grams):
    n, panel = grams[0].shape[0], 4
    count, groups = len(grams), n // 8
    sub = lax.broadcasted_iota(jnp.int32, (8, n), 0)
    lane = lax.broadcasted_iota(jnp.int32, (8, n), 1)
    left = [[g[8 * i : 8 * i + 8] for i in range(groups)] for g in grams]
    right = [[(lane == sub + 8 * i).astype(FULL) for i in range(groups)] for _ in grams]
    upper, lower = [[] for _ in grams], [[] for _ in grams]
    for p in range(groups):
        end = (p // panel + 1) * panel
        raw = [[[None] * 8 for _ in range(p, end)] for _ in grams]
        for some in (range(p, p + 1), range(p + 1, end)):
            for k in range(8):
                for t in range(count):
                    for g in some:
                        column = left[t][g][:, 8 * p + k : 8 * p + k + 1]
                        raw[t][g - p][k] = jnp.broadcast_to(column, (8, n))
        for t in range(count):
            a, b, col, pivots = left[t][p], right[t][p], list(raw[t][0]), None
            for k in range(8):
                pivot = spread(col[k], k)
                pivots = pivot if pivots is None else jnp.where(sub == k, pivot, pivots)
                if k < 7:
                    f = jnp.where(sub > k, col[k], 0.0) * (1.0 / pivot)
                    for i in range(k + 1, 8):
                        col[i] = col[i] - f * spread(col[i], k)
                    a, b = a - f * spread(a, k), b - f * spread(b, k)
            root = lax.rsqrt(pivots)
            upper[t].append(a * root)
            lower[t].append(b * root)
            if p + 1 < end:
                ratio = 1.0 / pivots
                y, z = a * ratio, b * ratio
                for i in range(7, 0, -1):
                    f = jnp.where(sub < i, col[i] * ratio, 0.0)
                    y, z = y - f * spread(y, i), z - f * spread(z, i)
                for g in range(p + 1, end):
                    for k in range(8):
                        c = raw[t][g - p][k]
                        left[t][g] = left[t][g] - c * spread(y, k)
                        right[t][g] = right[t][g] - c * spread(z, k)
        if p + 1 == end and end < groups:
            for t in range(count):
                ah, al = halves(jnp.concatenate(upper[t][end - panel :], 0))
                bh, bl = halves(jnp.concatenate(lower[t][end - panel :], 0))
                factor = jnp.concatenate([ah, ah, al], 0)
                cut_a = dot(factor, jnp.concatenate([ah, al, ah], 0), 0, 0)
                cut_b = dot(factor, jnp.concatenate([bh, bl, bh], 0), 0, 0)
                for g in range(end, groups):
                    left[t][g] = left[t][g] - cut_a[8 * g : 8 * g + 8]
                    right[t][g] = right[t][g] - cut_b[8 * g : 8 * g + 8]
    return [jnp.concatenate(rows, 0) for rows in lower]


def join_body(right_any, left_any, out_ref, sems):
    slots = right_any.shape[0]
    copies = [
        pltpu.make_async_copy(right_any, out_ref.at[:slots], sems.at[0]),
        pltpu.make_async_copy(left_any, out_ref.at[slots:], sems.at[1]),
    ]
    for c in copies:
        c.start()
    for c in copies:
        c.wait()


def probe_body(
    place_ref, left_any, sketch_any, out_ref, own_ref, left_ref, sketch_ref, sems, *, first
):
    count = out_ref.shape[0]
    copies = [pltpu.make_async_copy(sketch_any, sketch_ref, sems.at[count])]
    for k in range(count):
        copies.append(
            pltpu.make_async_copy(left_any.at[first + k], left_ref.at[k], sems.at[k])
        )
    for c in copies:
        c.start()
    copies[0].wait()
    lines = own_ref.shape[0]
    own_ref[...] = sketch_ref[pl.ds(pl.multiple_of(place_ref[4] * lines, lines), lines), :]
    for k in range(count):
        copies[1 + k].wait()
        for t in range(2):
            cols = slice(128 * t, 128 * t + 128)
            out_ref[k, t] = dot(left_ref[k, :, cols], sketch_ref[:, cols], 0, 0)


def early_body(place_ref, own, f1, b1, f2, b2, f3, b3, right_ref, pair_ref, pivot_ref, factor):
    group, groups, core = place_ref[0], place_ref[2], place_ref[3]
    slots, n = right_ref.shape[0], own.shape[1]

    def put(ref, distance):
        at = pl.multiple_of(lax.rem(group + distance, groups) * n, n)
        for k in range(slots):
            cols = slice(128 * k, 128 * k + 128)
            if ref is None:
                factor[pl.ds(at, n), cols] = jnp.zeros((n, 128), LOW)
                pivot_ref[pl.ds(at, n), cols] = jnp.zeros((n, 128), LOW)
            else:
                factor[pl.ds(at, n), cols] = ref[k]
                pivot_ref[pl.ds(at, n), cols] = ref[k + slots]

    put(own, 0)
    for s, (f, b) in enumerate(((f1, b1), (f2, b2), (f3, b3))):
        put(f, jnp.where(core == 0, groups - 1 - s, 1 + s))
        put(b, jnp.where(core == 0, 1 + s, groups - 1 - s))
    put(None, groups // 2)
    for k in range(slots):
        pair_ref[k] = dot(factor[:, 128 * k : 128 * k + 128], right_ref[k], 0, 0)


def upper_lines(shape):
    return lax.broadcasted_iota(jnp.int32, shape, 1) < 4


def packed(x):
    x = x.reshape(16, 8, 128)
    high = x.astype(LOW).astype(FULL)
    low, top = x - high, upper_lines(x.shape)
    even = jnp.where(top, high, pltpu.roll(low, 4, 1))
    odd = jnp.where(top, pltpu.roll(high, 4, 1), low)
    return jnp.concatenate([even[:, None], odd[:, None]], 1).reshape(32, 8, 128)


def repacked(x):
    total = x + pltpu.roll(x, 4, 1)
    high = total.astype(LOW).astype(FULL)
    return jnp.where(upper_lines(x.shape), high, total - high)


def unpacked(x):
    total = (x + pltpu.roll(x, 4, 1)).reshape(16, 2, 8, 128)
    even, odd = total[:, 0], total[:, 1]
    return jnp.where(upper_lines(even.shape), even, odd).reshape(128, 128)


def forward_body(
    place_ref, f4, b4, early_ref, pivot_ref, probe_low, probe_high, sketch_ref, right_ref, tright_ref,
    keep_ref, send_ref, pair_ref, part,
):
    group, live, groups, core = place_ref[0], place_ref[1], place_ref[2], place_ref[3]
    slots, n, half = right_ref.shape[0], f4.shape[1], keep_ref.shape[0]
    at = pl.multiple_of(lax.rem(group + groups // 2, groups) * n, n)
    mixed = []
    for k in range(slots):
        pair = early_ref[k] + dot(f4[k], right_ref[k, pl.ds(at, n), :], 0, 0)
        pair_ref[k] = pair
        row = []
        for t in range(2):
            cols = slice(128 * t, 128 * t + 128)
            probe = probe_low if k < probe_low.shape[0] else probe_high
            value = fine_dot(pair[:, cols], probe[k % probe_low.shape[0], t], 1, 0)
            row.append(jnp.where(k < live, -value, 0.0).astype(LOW))
        mixed.append(jnp.concatenate(row, 1))
    mixed = jnp.concatenate(mixed, 0)
    part[...] = dot(pivot_ref[...], mixed, 1, 0)
    last = jnp.concatenate([b4[k] for k in range(slots)], 1)
    part[pl.ds(at, n), :] = dot(last, mixed, 1, 0)
    cores = [
        dot(tright_ref[:, 128 * t : 128 * t + 128], sketch_ref[:, 128 * t : 128 * t + 128], 0, 0)
        for t in range(2)
    ]
    for t in range(2):
        whole = part[:, 128 * t : 128 * t + 128].reshape(half, 2, 16, 128)
        lines = slice(16 * t, 16 * t + 16)
        keep_ref[:, lines] = jnp.where(core == 0, whole[:, 0], whole[:, 1])
        send_ref[:, lines] = jnp.where(core == 0, whole[:, 1], whole[:, 0]).astype(LOW)
    keep_ref[:, 32:] = packed(jnp.where(core == 0, cores[0], cores[1]))
    send_ref[:, 32:] = packed(jnp.where(core == 0, cores[1], cores[0])).astype(LOW)


def add_body(keep_ref, come_ref, out_ref):
    out_ref[...] = (keep_ref[...] + come_ref[...].astype(FULL)).astype(LOW)


def last_body(pieces_ref, direct_ref, out_ref, *, rows):
    out_ref[...] = (jnp.sum(pieces_ref[...].astype(FULL), 0) + direct_ref[...]) / rows


def merge_body(keep_ref, come_ref, out_ref):
    total = keep_ref[...] + come_ref[...].astype(FULL)
    out_ref[:, :32] = total[:, :32].astype(LOW)
    out_ref[:, 32:] = repacked(total[:, 32:]).astype(LOW)


def own_body(pieces_ref, tleft_ref, sum_ref, out_ref):
    total = jnp.sum(pieces_ref[...].astype(FULL), 0)
    sum_ref[...] = jnp.concatenate([total[:16], total[16:32]], 1)
    lines = jnp.concatenate(
        [
            total[:32].astype(LOW),
            tleft_ref[:, :128],
            tleft_ref[:, 128:],
            repacked(total[None, 32:])[0].astype(LOW),
        ],
        0,
    )
    out_ref[...] = jnp.broadcast_to(lines[None], out_ref.shape)


def backward_body(
    place_ref, mine_ref, other_ref, own_ref, b4, pivot_ref, pair_ref, tleft_ref, tright_ref,
    left_ref, basis_ref, keep_ref, send_ref, direct_ref, turn_high, turn_low, tall,
):
    group, live, groups, core = place_ref[0], place_ref[1], place_ref[2], place_ref[3]
    slots, rows, n = left_ref.shape[0], tall.shape[0], b4.shape[1]

    def ordered(first):
        mine, other = mine_ref[:, first : first + 16], other_ref[:, first : first + 16]
        even, odd = jnp.where(core == 0, mine, other), jnp.where(core == 0, other, mine)
        return jnp.concatenate([even[:, None], odd[:, None]], 1).reshape(rows, -1)

    blocks = [mine_ref[:, 64:].astype(FULL), other_ref[:, 64:].astype(FULL)]
    at = pl.multiple_of(lax.rem(group + groups // 2, groups) * n, n)
    last = jnp.concatenate([b4[k] for k in range(slots)], 1)
    whole, own, grams, seen, seen_target = [], [], [], [], []
    for t in range(2):
        cols = slice(128 * t, 128 * t + 128)
        block = jnp.where(core == t, blocks[0], blocks[1])
        target_core = unpacked(block).astype(LOW)
        tall[:, cols] = ordered(32 + 16 * t)
        s = ordered(16 * t).astype(FULL) + dot(tall[:, cols], target_core, 1, 0)
        own.append(own_ref[:, cols] + dot(tleft_ref[:, cols], target_core, 1, 0))
        turned = s.T
        high, low = halves(turned)
        grams.append(dot(high, s.astype(LOW), 1, 0) / rows)
        turn_high[t] = high
        turn_low[t] = low
    for t in range(2):
        cols = slice(128 * t, 128 * t + 128)
        both = jnp.concatenate([turn_high[t], turn_low[t]], 0)
        product = dot(both, pivot_ref[...], 1, 0)
        tail = jnp.concatenate([turn_high[t, :, pl.ds(at, n)], turn_low[t, :, pl.ds(at, n)]], 0)
        product = product + dot(tail, last, 1, 0)
        seen.append(product[:128] + product[128:])
        product = dot(both, tall[:, cols], 1, 0)
        seen_target.append(product[:128] + product[128:])
    inverse = inverse_factors(grams)
    for t in range(2):
        cols = slice(128 * t, 128 * t + 128)
        basis_ref[:, cols] = fine_dot(own[t], inverse[t], 1, 1)
        back = fine_dot(inverse[t], seen[t], 1, 0)
        total = None
        for k in range(slots):
            folded = fine_dot(back[:, 128 * k : 128 * k + 128], pair_ref[k, :, cols], 1, 0)
            folded = jnp.where(k < live, -folded, 0.0).astype(LOW)
            term = dot(left_ref[k, :, cols], folded, 1, 1)
            total = term if total is None else total + term
        total = total.reshape(keep_ref.shape[0], 2, 16, 128)
        keep_ref[:, :, cols] = jnp.where(core == 0, total[:, 0], total[:, 1])
        send_ref[:, :, cols] = jnp.where(core == 0, total[:, 1], total[:, 0]).astype(LOW)
        target_back = fine_dot(inverse[t], seen_target[t], 1, 0).astype(LOW)
        direct_ref[:, cols] = dot(tright_ref[:, cols], target_back, 1, 1)


SMEM = pl.BlockSpec(memory_space=pltpu.SMEM)
VMEM = pl.BlockSpec(memory_space=pltpu.VMEM)


def shift(x, axis, by):
    n = lax.axis_size(axis)
    return lax.ppermute(x, axis, [(i, (i + by) % n) for i in range(n)])


def around(x, by):
    n = lax.axis_size("grp")
    pairs = [
        (2 * i + core, 2 * ((i + (by if core == 0 else -by)) % n) + core)
        for i in range(n)
        for core in range(2)
    ]
    return lax.ppermute(x, ("grp", INNER[2]), pairs)


def near(x):
    return pltpu.with_memory_space_constraint(x, pltpu.VMEM)


def kernel(body, name, outs, scratch, place, *arrays, given=(), leave=None):
    first = () if place is None else (place,)
    return pl.pallas_call(
        body,
        in_specs=[SMEM] * len(first) + [VMEM] * (len(arrays) + len(given)),
        out_specs=[VMEM] * len(outs),
        out_shape=[
            (jax.ShapeDtypeStruct if i == leave else pltpu.VMEM)(*o) for i, o in enumerate(outs)
        ],
        scratch_shapes=[pltpu.VMEM(*o) for o in scratch],
        name=name,
        compiler_params=pltpu.CompilerParams(vmem_limit_bytes=16 << 20),
    )(*first, *[near(x) for x in arrays], *given)


def probed(place, col_left, sketch_cols, block, first, count):
    return pl.pallas_call(
        functools.partial(probe_body, first=first),
        in_specs=[SMEM] + [pl.BlockSpec(memory_space=pltpu.HBM)] * 2,
        out_specs=[VMEM] * 2,
        out_shape=[
            pltpu.VMEM((count, 2, 128, 128), FULL),
            pltpu.VMEM((block, sketch_cols.shape[1]), LOW),
        ],
        scratch_shapes=[
            pltpu.VMEM((count, *col_left.shape[1:]), LOW),
            pltpu.VMEM(sketch_cols.shape, LOW),
            pltpu.SemaphoreType.DMA((count + 1,)),
        ],
        name="probe",
        compiler_params=pltpu.CompilerParams(vmem_limit_bytes=16 << 20),
    )(place, *(pltpu.with_memory_space_constraint(x, pltpu.HBM) for x in (col_left, sketch_cols)))


def shards(
    row_left, row_right, col_left, col_right, sketch_cols, target_left, target_right, live_counts
):
    slots, rows, width = col_left.shape
    block, factors = target_left.shape[0], slots * 128
    n, far, groups = lax.axis_size(INNER), INNER[:2], lax.axis_size("grp")
    half = n // 2
    place = jnp.stack(
        [
            lax.axis_index("grp"),
            live_counts[0],
            jnp.int32(groups),
            lax.axis_index(INNER[2]),
            lax.axis_index(INNER),
        ]
    ).astype(jnp.int32)
    own = pl.pallas_call(
        join_body,
        in_specs=[pl.BlockSpec(memory_space=pltpu.HBM)] * 2,
        out_specs=VMEM,
        out_shape=pltpu.VMEM((2 * slots, *row_left.shape[1:]), LOW),
        scratch_shapes=[pltpu.SemaphoreType.DMA((2,))],
        name="join",
        compiler_params=pltpu.CompilerParams(vmem_limit_bytes=16 << 20),
    )(*(pltpu.with_memory_space_constraint(x, pltpu.HBM) for x in (row_right, row_left)))
    chunks, probes, up, down = [own], [], own, own
    for step in range(3):
        up, down = around(up, 1), around(down, -1)
        if step:
            half_slots = slots // 2
            probe, own_sketch = probed(
                place, col_left, sketch_cols, block, (step - 1) * half_slots, half_slots
            )
            up, probe = lax.optimization_barrier((up, probe))
            probes.append(probe)
        chunks += [up, down]
    last_up, last_down = around(up[:slots], 1), around(down[slots:], -1)
    early, pivot = kernel(
        early_body,
        "early",
        [((slots, 128, width), FULL), ((rows, factors), LOW)],
        [((rows, factors), LOW)],
        place,
        *chunks,
        given=(col_right,),
    )
    piece = (half, block, width)
    keep, send, pair = kernel(
        forward_body,
        "forward",
        [((half, 40, 128), FULL), ((half, 40, 128), LOW), ((slots, 128, width), FULL)],
        [((rows, width), FULL)],
        place,
        last_up,
        last_down,
        early,
        pivot,
        *probes,
        own_sketch,
        given=(col_right, target_right),
    )
    (merged,) = kernel(
        merge_body, "merge", [((half, 40, 128), LOW)], [], None, keep, shift(send, INNER[2], 1)
    )
    own_sum, mine = kernel(
        own_body,
        "own",
        [((block, width), FULL), ((half, 72, 128), LOW)],
        [],
        None,
        lax.all_to_all(merged, far, 0, 0, tiled=True),
        given=(target_left,),
    )
    mine = lax.all_to_all(mine, far, 0, 0, tiled=True)
    other = shift(mine, INNER[2], 1)
    basis, keep, send, direct = kernel(
        backward_body,
        "backward",
        [((block, width), FULL), (piece, FULL), (piece, LOW), ((block, width), FULL)],
        [((2, 128, rows), LOW), ((2, 128, rows), LOW), ((rows, width), LOW)],
        place,
        mine,
        other,
        own_sum,
        last_down,
        pivot,
        pair,
        given=(target_left, target_right, col_left),
        leave=0,
    )
    (merged,) = kernel(add_body, "add", [(piece, LOW)], [], None, keep, shift(send, INNER[2], 1))
    merged = near(merged)
    (coeffs,) = kernel(
        functools.partial(last_body, rows=rows),
        "last",
        [((block, width), FULL)],
        [],
        None,
        lax.all_to_all(merged, far, 0, 0, tiled=True),
        direct,
        leave=0,
    )
    return basis, coeffs


def solution(mesh):
    finer = Mesh(
        mesh.devices.reshape(mesh.shape["grp"], 8, 4, 2), ("grp", "inner_0", "inner_1", "inner_2")
    )
    return jax.shard_map(
        shards,
        mesh=finer,
        in_specs=(
            P(INNER, "grp", None),
            P(INNER, "grp", None),
            P(INNER, None, "grp"),
            P(INNER, None, "grp"),
            P(None, "grp"),
            P(INNER, "grp"),
            P(INNER, "grp"),
            P(INNER),
        ),
        out_specs=(P(INNER, "grp"), P(INNER, "grp")),
        check_vma=False,
    )
```

```python
import functools

import jax
import jax.numpy as jnp
from jax import lax
from jax.experimental import pallas as pl
from jax.experimental.pallas import tpu as pltpu
from jax.sharding import Mesh
from jax.sharding import PartitionSpec as P

INNER = ("inner_0", "inner_1", "inner_2")
LOW = jnp.bfloat16
FULL = jnp.float32


def dot(a, b, ca, cb):
    return lax.dot_general(a, b, (((ca,), (cb,)), ((), ())), preferred_element_type=FULL)


def halves(x):
    high = x.astype(LOW)
    return high, (x - high.astype(FULL)).astype(LOW)


def fine_dot(a, b, ca, cb):
    ah, al = halves(a)
    bh, bl = halves(b)
    return dot(ah, bh, ca, cb) + (dot(ah, bl, ca, cb) + dot(al, bh, ca, cb))


def spread(x, i):
    return jnp.broadcast_to(x[i : i + 1, :], x.shape)


def inverse_factors(grams):
    n, panel = grams[0].shape[0], 4
    count, groups = len(grams), n // 8
    sub = lax.broadcasted_iota(jnp.int32, (8, n), 0)
    lane = lax.broadcasted_iota(jnp.int32, (8, n), 1)
    left = [[g[8 * i : 8 * i + 8] for i in range(groups)] for g in grams]
    right = [[(lane == sub + 8 * i).astype(FULL) for i in range(groups)] for _ in grams]
    upper, lower = [[] for _ in grams], [[] for _ in grams]
    for p in range(groups):
        end = (p // panel + 1) * panel
        raw = [[[None] * 8 for _ in range(p, end)] for _ in grams]
        for some in (range(p, p + 1), range(p + 1, end)):
            for k in range(8):
                for t in range(count):
                    for g in some:
                        column = left[t][g][:, 8 * p + k : 8 * p + k + 1]
                        raw[t][g - p][k] = jnp.broadcast_to(column, (8, n))
        for t in range(count):
            a, b, col, pivots = left[t][p], right[t][p], list(raw[t][0]), None
            for k in range(8):
                pivot = spread(col[k], k)
                pivots = pivot if pivots is None else jnp.where(sub == k, pivot, pivots)
                if k < 7:
                    f = jnp.where(sub > k, col[k], 0.0) * (1.0 / pivot)
                    for i in range(k + 1, 8):
                        col[i] = col[i] - f * spread(col[i], k)
                    a, b = a - f * spread(a, k), b - f * spread(b, k)
            root = lax.rsqrt(pivots)
            upper[t].append(a * root)
            lower[t].append(b * root)
            if p + 1 < end:
                ratio = 1.0 / pivots
                y, z = a * ratio, b * ratio
                for i in range(7, 0, -1):
                    f = jnp.where(sub < i, col[i] * ratio, 0.0)
                    y, z = y - f * spread(y, i), z - f * spread(z, i)
                for g in range(p + 1, end):
                    for k in range(8):
                        c = raw[t][g - p][k]
                        left[t][g] = left[t][g] - c * spread(y, k)
                        right[t][g] = right[t][g] - c * spread(z, k)
        if p + 1 == end and end < groups:
            for t in range(count):
                ah, al = halves(jnp.concatenate(upper[t][end - panel :], 0))
                bh, bl = halves(jnp.concatenate(lower[t][end - panel :], 0))
                factor = jnp.concatenate([ah, ah, al], 0)
                cut_a = dot(factor, jnp.concatenate([ah, al, ah], 0), 0, 0)
                cut_b = dot(factor, jnp.concatenate([bh, bl, bh], 0), 0, 0)
                for g in range(end, groups):
                    left[t][g] = left[t][g] - cut_a[8 * g : 8 * g + 8]
                    right[t][g] = right[t][g] - cut_b[8 * g : 8 * g + 8]
    return [jnp.concatenate(rows, 0) for rows in lower]


def join_body(right_any, left_any, out_ref, sems):
    slots = right_any.shape[0]
    copies = [
        pltpu.make_async_copy(right_any, out_ref.at[:slots], sems.at[0]),
        pltpu.make_async_copy(left_any, out_ref.at[slots:], sems.at[1]),
    ]
    for c in copies:
        c.start()
    for c in copies:
        c.wait()


def probe_body(
    place_ref, left_any, sketch_any, out_ref, own_ref, left_ref, sketch_ref, sems, *, first
):
    count = out_ref.shape[0]
    copies = [pltpu.make_async_copy(sketch_any, sketch_ref, sems.at[count])]
    for k in range(count):
        copies.append(
            pltpu.make_async_copy(left_any.at[first + k], left_ref.at[k], sems.at[k])
        )
    for c in copies:
        c.start()
    copies[0].wait()
    lines = own_ref.shape[0]
    own_ref[...] = sketch_ref[pl.ds(pl.multiple_of(place_ref[4] * lines, lines), lines), :]
    for k in range(count):
        copies[1 + k].wait()
        for t in range(2):
            cols = slice(128 * t, 128 * t + 128)
            out_ref[k, t] = dot(left_ref[k, :, cols], sketch_ref[:, cols], 0, 0)


def early_body(
    place_ref, own, f1, b1, f2, b2, f3, b3, sketch_ref, right_ref, tright_ref,
    pair_ref, pivot_ref, core_keep, core_send, factor,
):
    group, groups = place_ref[0], place_ref[2]
    slots, n = right_ref.shape[0], own.shape[1]

    def put(ref, distance):
        at = pl.multiple_of(lax.rem(group + distance, groups) * n, n)
        for k in range(slots):
            cols = slice(128 * k, 128 * k + 128)
            if ref is None:
                factor[pl.ds(at, n), cols] = jnp.zeros((n, 128), LOW)
                pivot_ref[pl.ds(at, n), cols] = jnp.zeros((n, 128), LOW)
            else:
                factor[pl.ds(at, n), cols] = ref[k]
                pivot_ref[pl.ds(at, n), cols] = ref[k + slots]

    put(own, 0)
    for s, (f, b) in enumerate(((f1, b1), (f2, b2), (f3, b3))):
        put(f, groups - 1 - s)
        put(b, 1 + s)
    put(None, groups // 2)
    for k in range(slots):
        pair_ref[k] = dot(factor[:, 128 * k : 128 * k + 128], right_ref[k], 0, 0)
    core = place_ref[3]
    cores = [
        dot(tright_ref[:, 128 * t : 128 * t + 128], sketch_ref[:, 128 * t : 128 * t + 128], 0, 0)
        for t in range(2)
    ]
    core_keep[...] = packed(jnp.where(core == 0, cores[0], cores[1]))
    core_send[...] = packed(jnp.where(core == 0, cores[1], cores[0]))


def upper_lines(shape):
    return lax.broadcasted_iota(jnp.int32, shape, 1) < 4


def packed(x):
    x = x.reshape(16, 8, 128)
    high = x.astype(LOW).astype(FULL)
    low, top = x - high, upper_lines(x.shape)
    even = jnp.where(top, high, pltpu.roll(low, 4, 1))
    odd = jnp.where(top, pltpu.roll(high, 4, 1), low)
    return jnp.concatenate([even[:, None], odd[:, None]], 1).reshape(32, 8, 128)


def repacked(x):
    total = x + pltpu.roll(x, 4, 1)
    high = total.astype(LOW).astype(FULL)
    return jnp.where(upper_lines(x.shape), high, total - high)


def unpacked(x):
    total = (x + pltpu.roll(x, 4, 1)).reshape(16, 2, 8, 128)
    even, odd = total[:, 0], total[:, 1]
    return jnp.where(upper_lines(even.shape), even, odd).reshape(128, 128)


def forward_body(
    place_ref, f4, b4, early_ref, pivot_ref, probe_low, probe_high, core_keep, core_send, right_ref,
    keep_ref, send_ref, pair_ref, part,
):
    group, live, groups, core = place_ref[0], place_ref[1], place_ref[2], place_ref[3]
    slots, n, half = right_ref.shape[0], f4.shape[1], keep_ref.shape[0]
    at = pl.multiple_of(lax.rem(group + groups // 2, groups) * n, n)
    mixed = []
    for k in range(slots):
        pair = early_ref[k] + dot(f4[k], right_ref[k, pl.ds(at, n), :], 0, 0)
        pair_ref[k] = pair
        row = []
        for t in range(2):
            cols = slice(128 * t, 128 * t + 128)
            probe = probe_low if k < probe_low.shape[0] else probe_high
            value = fine_dot(pair[:, cols], probe[k % probe_low.shape[0], t], 1, 0)
            row.append(jnp.where(k < live, -value, 0.0).astype(LOW))
        mixed.append(jnp.concatenate(row, 1))
    mixed = jnp.concatenate(mixed, 0)
    part[...] = dot(pivot_ref[...], mixed, 1, 0)
    last = jnp.concatenate([b4[k] for k in range(slots)], 1)
    part[pl.ds(at, n), :] = dot(last, mixed, 1, 0)
    for t in range(2):
        whole = part[:, 128 * t : 128 * t + 128].reshape(half, 2, 16, 128)
        lines = slice(16 * t, 16 * t + 16)
        keep_ref[:, lines] = jnp.where(core == 0, whole[:, 0], whole[:, 1])
        send_ref[:, lines] = jnp.where(core == 0, whole[:, 1], whole[:, 0]).astype(LOW)
    keep_ref[:, 32:] = core_keep[...]
    send_ref[:, 32:] = core_send[...].astype(LOW)


def add_body(keep_ref, come_ref, out_ref):
    out_ref[...] = (keep_ref[...] + come_ref[...].astype(FULL)).astype(LOW)


def last_body(pieces_ref, direct_ref, out_ref, *, rows):
    out_ref[...] = (jnp.sum(pieces_ref[...].astype(FULL), 0) + direct_ref[...]) / rows


def merge_body(keep_ref, come_ref, out_ref):
    total = keep_ref[...] + come_ref[...].astype(FULL)
    out_ref[:, :32] = total[:, :32].astype(LOW)
    out_ref[:, 32:] = repacked(total[:, 32:]).astype(LOW)


def own_body(pieces_ref, tleft_ref, sum_ref, out_ref):
    total = jnp.sum(pieces_ref[...].astype(FULL), 0)
    sum_ref[...] = jnp.concatenate([total[:16], total[16:32]], 1)
    lines = jnp.concatenate(
        [
            total[:32].astype(LOW),
            tleft_ref[:, :128],
            tleft_ref[:, 128:],
            repacked(total[None, 32:])[0].astype(LOW),
        ],
        0,
    )
    out_ref[...] = jnp.broadcast_to(lines[None], out_ref.shape)


def backward_body(
    place_ref, mine_ref, other_ref, own_ref, b4, pivot_ref, pair_ref, tleft_ref, tright_ref,
    left_ref, basis_ref, keep_ref, send_ref, direct_ref, turn_high, turn_low, tall,
):
    group, live, groups, core = place_ref[0], place_ref[1], place_ref[2], place_ref[3]
    slots, rows, n = left_ref.shape[0], tall.shape[0], b4.shape[1]

    def ordered(first):
        mine, other = mine_ref[:, first : first + 16], other_ref[:, first : first + 16]
        even, odd = jnp.where(core == 0, mine, other), jnp.where(core == 0, other, mine)
        return jnp.concatenate([even[:, None], odd[:, None]], 1).reshape(rows, -1)

    blocks = [mine_ref[:, 64:].astype(FULL), other_ref[:, 64:].astype(FULL)]
    at = pl.multiple_of(lax.rem(group + groups // 2, groups) * n, n)
    last = jnp.concatenate([b4[k] for k in range(slots)], 1)
    whole, own, grams, seen, seen_target = [], [], [], [], []
    for t in range(2):
        cols = slice(128 * t, 128 * t + 128)
        block = jnp.where(core == t, blocks[0], blocks[1])
        target_core = unpacked(block).astype(LOW)
        tall[:, cols] = ordered(32 + 16 * t)
        s = ordered(16 * t).astype(FULL) + dot(tall[:, cols], target_core, 1, 0)
        own.append(own_ref[:, cols] + dot(tleft_ref[:, cols], target_core, 1, 0))
        turned = s.T
        high, low = halves(turned)
        grams.append(dot(high, s.astype(LOW), 1, 0) / rows)
        turn_high[t] = high
        turn_low[t] = low
    for t in range(2):
        cols = slice(128 * t, 128 * t + 128)
        both = jnp.concatenate([turn_high[t], turn_low[t]], 0)
        product = dot(both, pivot_ref[...], 1, 0)
        tail = jnp.concatenate([turn_high[t, :, pl.ds(at, n)], turn_low[t, :, pl.ds(at, n)]], 0)
        product = product + dot(tail, last, 1, 0)
        seen.append(product[:128] + product[128:])
        product = dot(both, tall[:, cols], 1, 0)
        seen_target.append(product[:128] + product[128:])
    inverse = inverse_factors(grams)
    for t in range(2):
        cols = slice(128 * t, 128 * t + 128)
        basis_ref[:, cols] = fine_dot(own[t], inverse[t], 1, 1)
        back = fine_dot(inverse[t], seen[t], 1, 0)
        total = None
        for k in range(slots):
            folded = fine_dot(back[:, 128 * k : 128 * k + 128], pair_ref[k, :, cols], 1, 0)
            folded = jnp.where(k < live, -folded, 0.0).astype(LOW)
            term = dot(left_ref[k, :, cols], folded, 1, 1)
            total = term if total is None else total + term
        total = total.reshape(keep_ref.shape[0], 2, 16, 128)
        keep_ref[:, :, cols] = jnp.where(core == 0, total[:, 0], total[:, 1])
        send_ref[:, :, cols] = jnp.where(core == 0, total[:, 1], total[:, 0]).astype(LOW)
        target_back = fine_dot(inverse[t], seen_target[t], 1, 0).astype(LOW)
        direct_ref[:, cols] = dot(tright_ref[:, cols], target_back, 1, 1)


SMEM = pl.BlockSpec(memory_space=pltpu.SMEM)
VMEM = pl.BlockSpec(memory_space=pltpu.VMEM)


def shift(x, axis, by):
    n = lax.axis_size(axis)
    return lax.ppermute(x, axis, [(i, (i + by) % n) for i in range(n)])


def near(x):
    return pltpu.with_memory_space_constraint(x, pltpu.VMEM)


def kernel(body, name, outs, scratch, place, *arrays, given=(), leave=None):
    first = () if place is None else (place,)
    return pl.pallas_call(
        body,
        in_specs=[SMEM] * len(first) + [VMEM] * (len(arrays) + len(given)),
        out_specs=[VMEM] * len(outs),
        out_shape=[
            (jax.ShapeDtypeStruct if i == leave else pltpu.VMEM)(*o) for i, o in enumerate(outs)
        ],
        scratch_shapes=[pltpu.VMEM(*o) for o in scratch],
        name=name,
        compiler_params=pltpu.CompilerParams(vmem_limit_bytes=16 << 20),
    )(*first, *[near(x) for x in arrays], *given)


def probed(place, col_left, sketch_cols, block, first, count):
    return pl.pallas_call(
        functools.partial(probe_body, first=first),
        in_specs=[SMEM] + [pl.BlockSpec(memory_space=pltpu.HBM)] * 2,
        out_specs=[VMEM] * 2,
        out_shape=[
            pltpu.VMEM((count, 2, 128, 128), FULL),
            pltpu.VMEM((block, sketch_cols.shape[1]), LOW),
        ],
        scratch_shapes=[
            pltpu.VMEM((count, *col_left.shape[1:]), LOW),
            pltpu.VMEM(sketch_cols.shape, LOW),
            pltpu.SemaphoreType.DMA((count + 1,)),
        ],
        name="probe",
        compiler_params=pltpu.CompilerParams(vmem_limit_bytes=16 << 20),
    )(place, *(pltpu.with_memory_space_constraint(x, pltpu.HBM) for x in (col_left, sketch_cols)))


def shards(
    row_left, row_right, col_left, col_right, sketch_cols, target_left, target_right, live_counts
):
    slots, rows, width = col_left.shape
    block, factors = target_left.shape[0], slots * 128
    n, far, groups = lax.axis_size(INNER), INNER[:2], lax.axis_size("grp")
    half = n // 2
    place = jnp.stack(
        [
            lax.axis_index("grp"),
            live_counts[0],
            jnp.int32(groups),
            lax.axis_index(INNER[2]),
            lax.axis_index(INNER),
        ]
    ).astype(jnp.int32)
    own = pl.pallas_call(
        join_body,
        in_specs=[pl.BlockSpec(memory_space=pltpu.HBM)] * 2,
        out_specs=VMEM,
        out_shape=pltpu.VMEM((2 * slots, *row_left.shape[1:]), LOW),
        scratch_shapes=[pltpu.SemaphoreType.DMA((2,))],
        name="join",
        compiler_params=pltpu.CompilerParams(vmem_limit_bytes=16 << 20),
    )(*(pltpu.with_memory_space_constraint(x, pltpu.HBM) for x in (row_right, row_left)))
    chunks, probes, up, down = [own], [], own, own
    for step in range(3):
        up, down = shift(up, "grp", 1), shift(down, "grp", -1)
        if step:
            half_slots = slots // 2
            probe, own_sketch = probed(
                place, col_left, sketch_cols, block, (step - 1) * half_slots, half_slots
            )
            up, probe = lax.optimization_barrier((up, probe))
            probes.append(probe)
        chunks += [up, down]
    last_up, last_down = shift(up[:slots], "grp", 1), shift(down[slots:], "grp", -1)
    early, pivot, core_keep, core_send = kernel(
        early_body,
        "early",
        [((slots, 128, width), FULL), ((rows, factors), LOW)] + [((half, 8, 128), FULL)] * 2,
        [((rows, factors), LOW)],
        place,
        *chunks,
        own_sketch,
        given=(col_right, target_right),
    )
    piece = (half, block, width)
    keep, send, pair = kernel(
        forward_body,
        "forward",
        [((half, 40, 128), FULL), ((half, 40, 128), LOW), ((slots, 128, width), FULL)],
        [((rows, width), FULL)],
        place,
        last_up,
        last_down,
        early,
        pivot,
        *probes,
        core_keep,
        core_send,
        given=(col_right,),
    )
    (merged,) = kernel(
        merge_body, "merge", [((half, 40, 128), LOW)], [], None, keep, shift(send, INNER[2], 1)
    )
    own_sum, mine = kernel(
        own_body,
        "own",
        [((block, width), FULL), ((half, 72, 128), LOW)],
        [],
        None,
        lax.all_to_all(merged, far, 0, 0, tiled=True),
        given=(target_left,),
    )
    mine = lax.all_to_all(mine, far, 0, 0, tiled=True)
    other = shift(mine, INNER[2], 1)
    basis, keep, send, direct = kernel(
        backward_body,
        "backward",
        [((block, width), FULL), (piece, FULL), (piece, LOW), ((block, width), FULL)],
        [((2, 128, rows), LOW), ((2, 128, rows), LOW), ((rows, width), LOW)],
        place,
        mine,
        other,
        own_sum,
        last_down,
        pivot,
        pair,
        given=(target_left, target_right, col_left),
        leave=0,
    )
    (merged,) = kernel(add_body, "add", [(piece, LOW)], [], None, keep, shift(send, INNER[2], 1))
    merged = near(merged)
    (coeffs,) = kernel(
        functools.partial(last_body, rows=rows),
        "last",
        [((block, width), FULL)],
        [],
        None,
        lax.all_to_all(merged, far, 0, 0, tiled=True),
        direct,
        leave=0,
    )
    return basis, coeffs


def solution(mesh):
    finer = Mesh(
        mesh.devices.reshape(mesh.shape["grp"], 8, 4, 2), ("grp", "inner_0", "inner_1", "inner_2")
    )
    return jax.shard_map(
        shards,
        mesh=finer,
        in_specs=(
            P(INNER, "grp", None),
            P(INNER, "grp", None),
            P(INNER, None, "grp"),
            P(INNER, None, "grp"),
            P(None, "grp"),
            P(INNER, "grp"),
            P(INNER, "grp"),
            P(INNER),
        ),
        out_specs=(P(INNER, "grp"), P(INNER, "grp")),
        check_vma=False,
    )
```
